256 devices in a mesh: chan: 32 (over x_hi, z, core), bfly: 2 (over x_lo), samp: 4 (over y).
Axes of the slice: x: 4 (x_hi: 2, x_lo: 2; x = x_hi * 2 + x_lo), y: 4, z: 8, core: 2. Of those that a mesh axis runs over, the one named last changes fastest.
Arguments:
- features: bfloat16 [65536, 2048], P(('chan', 'bfly'), 'samp'), may hold values from -6 to 6
- cotangent: bfloat16 [65536, 2048], P(('chan', 'bfly'), 'samp'), may hold values from -6 to 6
- right_factor: bfloat16 [2, 256, 256, 256], P(None, ('chan', 'bfly')), may hold values from -0.375 to 0.375
- left_factor: float32 [2, 256, 256, 256], P(None, ('chan', 'bfly')), may hold values from -0.375 to 0.375
- mixing: float32 [2, 2, 256, 256], P(None, None, ('chan', 'bfly')), may hold values from -1.2 to 1.2
Outputs:
- output: bfloat16 [65536, 2048], P(('chan', 'bfly'), 'samp')
- feature_grad: bfloat16 [65536, 2048], P(('chan', 'bfly'), 'samp')
- grad_right: float32 [2, 256, 256, 256], P(None, ('chan', 'bfly'))
- grad_left: float32 [2, 256, 256, 256], P(None, ('chan', 'bfly'))
- grad_mixing: float32 [2, 2, 256, 256], P(None, None, ('chan', 'bfly'))
The draws below stay inside these ranges and needn't reach their ends.
All inputs are finite; a program needn't handle non-finite values.
Results may differ from the reference program's by a relative error of at most 0.025.
Values may be sent and summed in bfloat16 or wider, within the bound.
A program may use at most 128 MiB of HBM per device.

```python
import jax
import jax.numpy as jnp
from jax import lax

BLOCK = 256
LAYERS = 2
SAMP_DEV = 512
WIDTH = 65536
SAMPLES = 2048
BLK_DEV = 4


def shard_levels(key, dims, pieces, smallest, top_value):
    loudness = 1.0
    for dim, parts in pieces:
        draws = jax.random.uniform(jax.random.fold_in(jax.random.fold_in(key, 6), dim), (parts,), jnp.float32, smallest / len(pieces), top_value / len(pieces))
        loudness = loudness * jnp.repeat(jnp.exp(draws), dims[dim] // parts).reshape((-1,) + (1,) * (len(dims) - 1 - dim))
    return loudness


def centred(rng, dims, width, reach, split=(), kind=jnp.bfloat16):
    factor_of = shard_levels(rng, dims, split, -0.22, 0.18) if split else 1.0
    result = jax.random.normal(rng, dims, jnp.float32) * width * factor_of
    return jnp.minimum(jnp.maximum(result, -reach), reach).astype(kind)


def setup_inputs(seed: int = 0) -> dict:
    splits = jax.random.split(jax.random.key(seed), 6)
    return {
        "features": centred(splits[0], (WIDTH, SAMPLES), 1.0, 6.0, ((0, 64), (1, 4))),
        "cotangent": centred(splits[1], (WIDTH, SAMPLES), 1.0, 6.0, ((0, 64), (1, 4))),
        "right_factor": centred(splits[2], (LAYERS, BLOCK, BLOCK, BLOCK), BLOCK ** -0.5, 0.375, ((1, 64),)),
        "left_factor": centred(splits[3], (LAYERS, BLOCK, BLOCK, BLOCK), BLOCK ** -0.5, 0.375, ((1, 64),), jnp.float32),
        "mixing": jnp.clip(jax.random.uniform(splits[4], (LAYERS, 2, BLOCK, BLOCK), jnp.float32, -1.2, 1.2) * shard_levels(splits[4], (LAYERS, 2, BLOCK, BLOCK), ((2, 64),), -0.4, 0.0), -1.2, 1.2),
    }


def flip_pairs(values, span):
    shape = values.shape
    grouped = values.reshape((shape[0] // (2 * span), 2, span) + shape[1:])
    return grouped[:, ::-1].reshape(shape)


def run_block(features, cotangent, right_factor, left_factor, mixing):
    samples = features.shape[1]
    height = features.reshape(BLOCK, BLOCK, samples)
    saved = []
    for layer_index in range(LAYERS):
        right_full = right_factor[layer_index].astype(jnp.float32)
        left_full = left_factor[layer_index].astype(jnp.float32)
        self_gain = mixing[layer_index, 0][:, :, None]
        cross_gain = mixing[layer_index, 1][:, :, None]
        mixed_u = jnp.einsum('bis,bij->bjs', height.astype(jnp.float32), right_full).astype(jnp.bfloat16)
        partner = flip_pairs(mixed_u, BLK_DEV)
        mixed_v = (self_gain * mixed_u.astype(jnp.float32) + cross_gain * partner.astype(jnp.float32)).astype(jnp.bfloat16)
        outer = jnp.einsum('bjs,jbk->kjs', mixed_v.astype(jnp.float32), left_full).astype(jnp.bfloat16)
        saved.append((height, mixed_u, partner, mixed_v, outer))
        height = (height.astype(jnp.float32) + jax.nn.silu(outer.astype(jnp.float32))).astype(jnp.bfloat16)
    output = height.reshape(WIDTH, samples)
    grad = cotangent.reshape(BLOCK, BLOCK, samples)
    rights = [None] * LAYERS
    lefts = [None] * LAYERS
    mixes = [None] * LAYERS
    for layer_index in reversed(range(LAYERS)):
        height_in, mixed_u, partner, mixed_v, outer = saved[layer_index]
        right_full = right_factor[layer_index].astype(jnp.float32)
        left_full = left_factor[layer_index].astype(jnp.float32)
        self_gain = mixing[layer_index, 0][:, :, None]
        cross_gain = mixing[layer_index, 1][:, :, None]
        before = outer.astype(jnp.float32)
        logistic = jax.nn.sigmoid(before)
        error = (grad.astype(jnp.float32) * logistic * (1.0 + before * (1.0 - logistic))).astype(jnp.bfloat16)
        error_full = error.astype(jnp.float32)
        lefts[layer_index] = jnp.einsum('bjs,kjs->jbk', mixed_v.astype(jnp.float32), error_full)
        grad_v = jnp.einsum('jbk,kjs->bjs', left_full, error_full).astype(jnp.bfloat16)
        grad_vf = grad_v.astype(jnp.float32)
        mixes[layer_index] = jnp.stack([jnp.sum(grad_vf * mixed_u.astype(jnp.float32), axis=2), jnp.sum(grad_vf * partner.astype(jnp.float32), axis=2)])
        carried = lax.optimization_barrier((cross_gain * grad_vf).astype(jnp.bfloat16))
        grad_u = (self_gain * grad_vf + flip_pairs(carried, BLK_DEV).astype(jnp.float32)).astype(jnp.bfloat16)
        grad_uf = grad_u.astype(jnp.float32)
        rights[layer_index] = jnp.einsum('bis,bjs->bij', height_in.astype(jnp.float32), grad_uf)
        grad = (grad.astype(jnp.float32) + jnp.einsum('bij,bjs->bis', right_full, grad_uf)).astype(jnp.bfloat16)
    return output, grad.reshape(WIDTH, samples), (jnp.stack(rights), jnp.stack(lefts), jnp.stack(mixes))


def reference(features, cotangent, right_factor, left_factor, mixing):
    count = features.shape[1] // SAMP_DEV

    def one_block(carry, index):
        start = (index * SAMP_DEV).astype(jnp.int32)
        feat_block = lax.dynamic_slice_in_dim(features, start, SAMP_DEV, 1)
        cot_block = lax.dynamic_slice_in_dim(cotangent, start, SAMP_DEV, 1)
        out_block, grad_block, grads = run_block(feat_block, cot_block, right_factor, left_factor, mixing)
        carry = (carry[0] + grads[0], carry[1] + grads[1], carry[2] + grads[2])
        return carry, (out_block, grad_block)

    start_sums = (jnp.zeros((LAYERS, BLOCK, BLOCK, BLOCK), jnp.float32), jnp.zeros((LAYERS, BLOCK, BLOCK, BLOCK), jnp.float32), jnp.zeros((LAYERS, 2, BLOCK, BLOCK), jnp.float32))
    sums, stacked = lax.scan(one_block, start_sums, jnp.arange(count, dtype=jnp.int32))
    output = jnp.transpose(stacked[0], (1, 0, 2)).reshape(WIDTH, count * SAMP_DEV)
    feature_grad = jnp.transpose(stacked[1], (1, 0, 2)).reshape(WIDTH, count * SAMP_DEV)
    return output, feature_grad, sums[0], sums[1], sums[2]
```

```python
import jax
import jax.numpy as jnp
from jax import lax
from jax.sharding import PartitionSpec as P

BLOCK = 256
LAYERS = 2


def flip(values):
    grouped = values.reshape((BLOCK // 8, 2, 4) + values.shape[1:])
    return grouped[:, ::-1].reshape(values.shape)


def to_columns(values):
    return lax.all_to_all(values, ("chan", "bfly"), split_axis=1, concat_axis=0, tiled=True)


def to_rows(values):
    return lax.all_to_all(values, ("chan", "bfly"), split_axis=0, concat_axis=1, tiled=True)


def local(features, cotangent, right_factor, left_factor, mixing):
    blocks = right_factor.shape[1]
    samples = features.shape[1]
    height = features.reshape(blocks, BLOCK, samples)
    mixing = lax.all_to_all(mixing, ("chan", "bfly"), split_axis=3, concat_axis=2, tiled=True)
    saved = []
    for layer_index in range(LAYERS):
        mixed_u = jnp.einsum(
            "bis,bij->bjs", height, right_factor[layer_index], preferred_element_type=jnp.float32
        ).astype(jnp.bfloat16)
        self_gain = mixing[layer_index, 0][:, :, None]
        cross_gain = mixing[layer_index, 1][:, :, None]
        mixed_u = to_columns(mixed_u)
        partner = flip(mixed_u)
        columns = (self_gain * mixed_u + cross_gain * partner).astype(jnp.bfloat16)
        kept = (mixed_u, partner)
        outer = jnp.einsum(
            "bjs,jbk->kjs", columns, left_factor[layer_index], preferred_element_type=jnp.float32
        ).astype(jnp.bfloat16)
        activation = to_rows(outer)
        saved.append((height, kept, columns, activation))
        height = (height.astype(jnp.float32) + jax.nn.silu(activation.astype(jnp.float32))).astype(
            jnp.bfloat16
        )
    output = height.reshape(blocks * BLOCK, samples)
    grad = cotangent.reshape(blocks, BLOCK, samples)
    rights = [None] * LAYERS
    lefts = [None] * LAYERS
    mixes = [None] * LAYERS
    for layer_index in reversed(range(LAYERS)):
        height_in, kept, columns, activation = saved[layer_index]
        before = activation.astype(jnp.float32)
        logistic = jax.nn.sigmoid(before)
        error = (grad.astype(jnp.float32) * logistic * (1.0 + before * (1.0 - logistic))).astype(
            jnp.bfloat16
        )
        error_cols = to_columns(error)
        grad_left = jnp.einsum(
            "bjs,kjs->jbk", columns, error_cols, preferred_element_type=jnp.float32
        )
        grad_cols = jnp.einsum(
            "jbk,kjs->bjs", left_factor[layer_index], error_cols, preferred_element_type=jnp.float32
        ).astype(jnp.bfloat16)
        mixed_u, partner = kept
        self_gain = mixing[layer_index, 0][:, :, None]
        cross_gain = mixing[layer_index, 1][:, :, None]
        grad_v = grad_cols
        grad_mix = jnp.stack(
            [
                jnp.einsum("bjs,bjs->bj", grad_v, mixed_u, preferred_element_type=jnp.float32),
                jnp.einsum("bjs,bjs->bj", grad_v, partner, preferred_element_type=jnp.float32),
            ]
        )
        carried = (cross_gain * grad_v).astype(jnp.bfloat16)
        returned = flip(carried)
        grad_u = to_rows((self_gain * grad_v + returned.astype(jnp.float32)).astype(jnp.bfloat16))
        grad_right = jnp.einsum(
            "bis,bjs->bij", height_in, grad_u, preferred_element_type=jnp.float32
        )
        back_term = jnp.einsum(
            "bij,bjs->bis", right_factor[layer_index], grad_u, preferred_element_type=jnp.float32
        )
        grad = (grad.astype(jnp.float32) + back_term).astype(jnp.bfloat16)
        rights[layer_index] = grad_right
        lefts[layer_index] = grad_left
        mixes[layer_index] = grad_mix
    all_right = jnp.stack(rights)
    all_left = jnp.stack(lefts)
    all_mix = lax.all_to_all(
        jnp.stack(mixes), ("chan", "bfly"), split_axis=2, concat_axis=3, tiled=True
    )
    all_right, all_left, all_mix = (
        lax.psum(all_right.astype(jnp.bfloat16), "samp").astype(jnp.float32),
        lax.psum(all_left.astype(jnp.bfloat16), "samp").astype(jnp.float32),
        lax.psum(all_mix.astype(jnp.bfloat16), "samp").astype(jnp.float32),
    )
    return (output, grad.reshape(blocks * BLOCK, samples), all_right, all_left, all_mix)


def solution(mesh):
    in_specs = (
        P(("chan", "bfly"), "samp"),
        P(("chan", "bfly"), "samp"),
        P(None, ("chan", "bfly"), None, None),
        P(None, ("chan", "bfly"), None, None),
        P(None, None, ("chan", "bfly"), None),
    )
    out_specs = (
        P(("chan", "bfly"), "samp"),
        P(("chan", "bfly"), "samp"),
        P(None, ("chan", "bfly"), None, None),
        P(None, ("chan", "bfly"), None, None),
        P(None, None, ("chan", "bfly"), None),
    )
    return jax.shard_map(local, mesh=mesh, in_specs=in_specs, out_specs=out_specs, check_vma=False)
```

```python
import functools

import jax
import jax.numpy as jnp
from jax import lax
from jax.experimental import pallas as pl
from jax.experimental.pallas import tpu as pltpu
from jax.sharding import PartitionSpec as P

BLOCK = 256
LAYERS = 2
PEERS = 64
OWN = 4
ROWS = 16
GROUPS = 4
GPEERS = PEERS // GROUPS
SAMP = 4
CHUNKS = 2
MESH = pl.DeviceIdType.MESH
F32 = jnp.float32
BF16 = jnp.bfloat16

U1, T1, U2, COT, T2, DU2, E1, DU1 = range(8)
GL2, GR2, GL1, GR1 = range(4)
Q_ROW, Q_ROW_T, Q_COL, Q_COL_T = range(4)


def mm(a, b):
    return lax.dot_general(a, b, (((1,), (0,)), ((), ())), preferred_element_type=F32)


def mm_t(a, b):
    return lax.dot_general(a, b, (((1,), (1,)), ((), ())), preferred_element_type=F32)


def flip(groups):
    parts = []
    for pair in range(GPEERS // 2):
        parts += [groups[2 * pair + 1 : 2 * pair + 2], groups[2 * pair : 2 * pair + 1]]
    return jnp.concatenate(parts, axis=0)


def kernel(
    feat, cot, right, left, mixing,
    out_hbm, fgrad_hbm, gright_hbm, gleft_hbm, gmix_ref,
    sendb, recvb, qmat, rt, lb, lt, h1, t1, vn, g1, nat, nat2, dvp, coef, outb, fgradb,
    mixs, mixr, gmacc, gms, gm1, gmy, gacc, gsend, rsr, ag,
    a_send, a_recv, m_send, m_recv, r_send, r_recv, g_send, g_recv, o_sem,
):
    samples = h1.shape[3]
    me = lax.axis_index("chan") * 2 + lax.axis_index("bfly")
    y = lax.axis_index("samp")

    def peer_id(p):
        return {"chan": p // 2, "bfly": lax.rem(p, 2)}

    barrier = pltpu.get_barrier_semaphore()

    def greet(k, carry):
        pl.semaphore_signal(barrier, inc=1, device_id=peer_id(lax.rem(me + k, PEERS)), device_id_type=MESH)
        return carry

    lax.fori_loop(1, PEERS, greet, 0)
    for d in range(1, SAMP):
        pl.semaphore_signal(barrier, inc=1, device_id={"samp": lax.rem(y + d, SAMP)}, device_id_type=MESH)

    i0 = lax.broadcasted_iota(jnp.int32, (BLOCK, BLOCK), 0)
    i1 = lax.broadcasted_iota(jnp.int32, (BLOCK, BLOCK), 1)

    def row_of(m):
        return ((m >> 2) & 3) * 64 + (m >> 4) * 4 + (m & 3)

    def col_of(m):
        return (m & 3) * 64 + (m >> 4) * 4 + ((m >> 2) & 3)

    def onehot(mask):
        return jnp.where(mask, 1.0, 0.0).astype(BF16)

    qmat[Q_ROW] = onehot(i1 == row_of(i0))
    qmat[Q_ROW_T] = onehot(i0 == row_of(i1))
    qmat[Q_COL] = onehot(i1 == col_of(i0))
    qmat[Q_COL_T] = onehot(i0 == col_of(i1))

    def to_peers(which, src, put):
        for g in range(GROUPS):
            x = jnp.concatenate([src[b, 64 * g : 64 * g + 64, :] for b in range(OWN)], axis=0)
            put(g, mm(qmat[which], x))

    def put_into(dst):
        def put(g, value):
            dst[GPEERS * g : GPEERS * (g + 1)] = value.astype(BF16).reshape(GPEERS, ROWS, samples)

        return put

    def split_into(dst, g, value):
        value = value.astype(BF16)
        for b in range(OWN):
            dst[b, 64 * g : 64 * g + 64, :] = value[64 * b : 64 * b + 64]

    def from_peers(which, src, dst):
        for g in range(GROUPS):
            x = src[GPEERS * g : GPEERS * (g + 1)].reshape(BLOCK, samples)
            split_into(dst, g, mm(qmat[which], x))

    def chunk_of(c):
        return pl.ds(pl.multiple_of(c * samples, samples), samples)

    def send(a, c):
        def one(k, carry):
            p = lax.rem(me + k, PEERS)
            pltpu.make_async_remote_copy(
                src_ref=sendb.at[a, c, p], dst_ref=recvb.at[a, c, me],
                send_sem=a_send.at[a, c], recv_sem=a_recv.at[a, c],
                device_id=peer_id(p), device_id_type=MESH,
            ).start()
            return carry

        lax.fori_loop(1, PEERS, one, 0)
        recvb[a, c, pl.ds(me, 1)] = sendb[a, c, pl.ds(me, 1)]

    def wait_all(ref, sem):
        pltpu.make_async_copy(ref, ref, sem).wait()

    def wait_recv(a, c):
        wait_all(recvb.at[a, c, pl.ds(0, PEERS - 1)], a_recv.at[a, c])

    pick = onehot((lax.broadcasted_iota(jnp.int32, (BLOCK, 128), 0) & 3) == (lax.broadcasted_iota(jnp.int32, (BLOCK, 128), 1) & 3)).astype(F32)
    lane = lax.broadcasted_iota(jnp.int32, (PEERS, 128), 1)
    owner = lax.broadcasted_iota(jnp.int32, (PEERS, BLOCK), 0)
    unit = lax.broadcasted_iota(jnp.int32, (PEERS, BLOCK), 1)
    message = jnp.zeros((PEERS, 128), F32)
    for r in range(ROWS):
        row = mixing[r // 8, (r // 4) % 2, r % 4 : r % 4 + 1, :]
        spread = jnp.where((unit >> 2) == owner, jnp.broadcast_to(row, (PEERS, BLOCK)), 0.0)
        found = lax.dot_general(
            spread, pick, (((1,), (0,)), ((), ())), precision=lax.Precision.HIGHEST, preferred_element_type=F32
        )
        message = message + jnp.where((lane >> 2) == r, found, 0.0)
    mixs[...] = message.reshape(PEERS, 1, 128)

    def prepare(layer):
        for b in range(OWN):
            rt[layer, b] = right[layer, b].T
            lb[layer, b] = left[layer, b].astype(BF16)
            lt[layer, b] = left[layer, b].T.astype(BF16)

    prepare(0)

    def first(c, carry):
        for b in range(OWN):
            nat[b] = mm(rt[0, b], feat[b, :, chunk_of(c)]).astype(BF16)
        to_peers(Q_ROW, nat, put_into(sendb.at[U1, c]))
        for b in range(OWN):
            nat[b] = cot[b, :, chunk_of(c)]
        to_peers(Q_ROW, nat, put_into(sendb.at[COT, c]))
        return carry

    lax.fori_loop(0, CHUNKS, first, 0)

    pl.semaphore_wait(barrier, PEERS - 1 + SAMP - 1)

    def send_mix(k, carry):
        p = lax.rem(me + k, PEERS)
        pltpu.make_async_remote_copy(
            src_ref=mixs.at[p], dst_ref=mixr.at[me], send_sem=m_send.at[0], recv_sem=m_recv.at[0],
            device_id=peer_id(p), device_id_type=MESH,
        ).start()
        return carry

    lax.fori_loop(1, PEERS, send_mix, 0)
    mixr[pl.ds(me, 1)] = mixs[pl.ds(me, 1)]
    for c in range(CHUNKS):
        send(U1, c)
    prepare(1)
    for a in range(4):
        gacc[a] = jnp.zeros((OWN, BLOCK, BLOCK), F32)
    gmacc[...] = jnp.zeros((PEERS, 128), F32)
    wait_all(mixr.at[pl.ds(0, PEERS - 1)], m_recv.at[0])
    lane3 = lax.broadcasted_iota(jnp.int32, (GPEERS, ROWS, 128), 2)
    row3 = lax.broadcasted_iota(jnp.int32, (GPEERS, ROWS, 128), 1)
    for g in range(GROUPS):
        got = jnp.broadcast_to(mixr[GPEERS * g : GPEERS * (g + 1)], (GPEERS, ROWS, 128))
        for term in range(4):
            value = jnp.sum(jnp.where(lane3 == row3 + ROWS * term, got, 0.0), axis=2, keepdims=True)
            coef[term, GPEERS * g : GPEERS * (g + 1)] = jnp.broadcast_to(value, (GPEERS, ROWS, 128))

    def gain(term, g):
        value = coef[term, GPEERS * g : GPEERS * (g + 1)]
        return jnp.concatenate([value] * (samples // 128), axis=2)

    def mix_forward(layer, a, c):
        for g in range(GROUPS):
            u = recvb[a, c, GPEERS * g : GPEERS * (g + 1)].astype(F32)
            v = (gain(2 * layer, g) * u + gain(2 * layer + 1, g) * flip(u)).astype(BF16)
            split_into(vn.at[layer, c], g, mm(qmat[Q_COL_T], v.reshape(BLOCK, samples)))

    def mix_backward(layer, a, c):
        def put(g, value):
            dv = value.reshape(GPEERS, ROWS, samples)
            dvp[GPEERS * g : GPEERS * (g + 1)] = dv.astype(BF16)
            part = (gain(2 * layer + 1, g) * dv).astype(BF16).astype(F32)
            du = gain(2 * layer, g) * dv + flip(part)
            sendb[a, c, GPEERS * g : GPEERS * (g + 1)] = du.astype(BF16)

        to_peers(Q_COL, nat2, put)

    def mix_gradient(layer, a, c):
        for g in range(GROUPS):
            dv = dvp[GPEERS * g : GPEERS * (g + 1)].astype(F32)
            u = recvb[a, c, GPEERS * g : GPEERS * (g + 1)].astype(F32)
            total = jnp.zeros((GPEERS, ROWS, 128), F32)
            for term, other in ((0, u), (1, flip(u))):
                prod = dv * other
                half = prod[:, :, :128]
                for piece in range(1, samples // 128):
                    half = half + prod[:, :, 128 * piece : 128 * (piece + 1)]
                value = jnp.sum(half, axis=2, keepdims=True)
                total = total + jnp.where(
                    lane3 == row3 + ROWS * (2 * layer + term), jnp.broadcast_to(value, (GPEERS, ROWS, 128)), 0.0
                )
            gmacc[GPEERS * g : GPEERS * (g + 1)] += jnp.sum(total, axis=1)

    def scatter(a):
        gsend[a] = gacc[a].astype(BF16)
        for d in range(1, SAMP):
            to = lax.rem(y + d, SAMP)
            pltpu.make_async_remote_copy(
                src_ref=gsend.at[a, to], dst_ref=rsr.at[a, y], send_sem=r_send.at[a], recv_sem=r_recv.at[a],
                device_id={"samp": to}, device_id_type=MESH,
            ).start()

    def gather(a):
        wait_all(rsr.at[a, pl.ds(0, SAMP - 1)], r_recv.at[a])
        total = gacc[a, y]
        for d in range(1, SAMP):
            total = total + rsr[a, lax.rem(y + d, SAMP)].astype(F32)
        ag[a, y] = total.astype(BF16)
        for d in range(1, SAMP):
            to = lax.rem(y + d, SAMP)
            pltpu.make_async_remote_copy(
                src_ref=ag.at[a, y], dst_ref=ag.at[a, y], send_sem=g_send.at[a], recv_sem=g_recv.at[a],
                device_id={"samp": to}, device_id_type=MESH,
            ).start()

    def store(a):
        wait_all(ag.at[a, pl.ds(0, SAMP - 1)], g_recv.at[a])
        dst = (gleft_hbm if a in (GL1, GL2) else gright_hbm).at[0 if a in (GL1, GR1) else 1]
        pltpu.make_async_copy(ag.at[a], dst, o_sem.at[a]).start()

    def col1(c, carry):
        wait_recv(U1, c)
        mix_forward(0, U1, c)
        for j in range(OWN):
            nat[j] = mm(lt[0, j], vn[0, c, j]).astype(BF16)
        to_peers(Q_COL, nat, put_into(sendb.at[T1, c]))
        send(T1, c)
        send(COT, c)
        return carry

    lax.fori_loop(0, CHUNKS, col1, 0)

    def row2(c, carry):
        wait_recv(T1, c)
        from_peers(Q_ROW_T, recvb.at[T1, c], t1.at[c])
        for b in range(OWN):
            t = t1[c, b].astype(F32)
            h = (feat[b, :, chunk_of(c)].astype(F32) + t * jax.nn.sigmoid(t)).astype(BF16)
            h1[c, b] = h
            nat[b] = mm(rt[1, b], h).astype(BF16)
        to_peers(Q_ROW, nat, put_into(sendb.at[U2, c]))
        send(U2, c)
        return carry

    lax.fori_loop(0, CHUNKS, row2, 0)

    def slope(g, t):
        s = jax.nn.sigmoid(t)
        return (g * s * (1.0 + t * (1.0 - s))).astype(BF16)

    def col2(c, carry):
        wait_recv(COT, c)
        from_peers(Q_COL_T, recvb.at[COT, c], nat2)
        wait_recv(U2, c)
        mix_forward(1, U2, c)
        for j in range(OWN):
            t = mm(lt[1, j], vn[1, c, j]).astype(BF16)
            nat[j] = t
            e = slope(nat2[j].astype(F32), t.astype(F32))
            gacc[GL2, j] += mm_t(vn[1, c, j], e)
            nat2[j] = mm(lb[1, j], e).astype(BF16)
        mix_backward(1, DU2, c)
        send(DU2, c)
        to_peers(Q_COL, nat, put_into(sendb.at[T2, c]))
        send(T2, c)
        mix_gradient(1, U2, c)
        return carry

    lax.fori_loop(0, CHUNKS, col2, 0)
    scatter(GL2)

    def row1(c, carry):
        wait_recv(DU2, c)
        from_peers(Q_ROW_T, recvb.at[DU2, c], nat)
        for b in range(OWN):
            g = (cot[b, :, chunk_of(c)].astype(F32) + mm(right[1, b], nat[b])).astype(BF16)
            g1[c, b] = g
            nat2[b] = slope(g.astype(F32), t1[c, b].astype(F32))
        to_peers(Q_ROW, nat2, put_into(sendb.at[E1, c]))
        send(E1, c)
        for b in range(OWN):
            gacc[GR2, b] += mm_t(h1[c, b], nat[b])
        return carry

    lax.fori_loop(0, CHUNKS, row1, 0)
    gather(GL2)
    scatter(GR2)

    def final_output(c, carry):
        wait_recv(T2, c)
        from_peers(Q_ROW_T, recvb.at[T2, c], nat)
        for b in range(OWN):
            t = nat[b].astype(F32)
            outb[b, :, chunk_of(c)] = (h1[c, b].astype(F32) + t * jax.nn.sigmoid(t)).astype(BF16)
        return carry

    lax.fori_loop(0, CHUNKS, final_output, 0)
    pltpu.make_async_copy(outb, out_hbm, o_sem.at[4]).start()

    def col1_back(c, carry):
        wait_recv(E1, c)
        from_peers(Q_COL_T, recvb.at[E1, c], nat)
        for j in range(OWN):
            nat2[j] = mm(lb[0, j], nat[j]).astype(BF16)
        mix_backward(0, DU1, c)
        send(DU1, c)
        for j in range(OWN):
            gacc[GL1, j] += mm_t(vn[0, c, j], nat[j])
        mix_gradient(0, U1, c)
        return carry

    lax.fori_loop(0, CHUNKS, col1_back, 0)
    scatter(GL1)
    gms[...] = gmacc[...].reshape(PEERS, 1, 128)

    def send_gm(k, carry):
        p = lax.rem(me + k, PEERS)
        pltpu.make_async_remote_copy(
            src_ref=gms.at[p], dst_ref=gm1.at[me], send_sem=m_send.at[1], recv_sem=m_recv.at[1],
            device_id=peer_id(p), device_id_type=MESH,
        ).start()
        return carry

    lax.fori_loop(1, PEERS, send_gm, 0)
    gm1[pl.ds(me, 1)] = gms[pl.ds(me, 1)]
    gather(GR2)
    store(GL2)
    wait_all(gm1.at[pl.ds(0, PEERS - 1)], m_recv.at[1])
    gmy[pl.ds(y, 1)] = gm1[...].reshape(1, PEERS, 1, 128)
    for d in range(1, SAMP):
        to = lax.rem(y + d, SAMP)
        pltpu.make_async_remote_copy(
            src_ref=gm1, dst_ref=gmy.at[y], send_sem=r_send.at[4], recv_sem=r_recv.at[4],
            device_id={"samp": to}, device_id_type=MESH,
        ).start()
    gather(GL1)
    store(GR2)

    def row0(c, carry):
        wait_recv(DU1, c)
        from_peers(Q_ROW_T, recvb.at[DU1, c], dun.at[c])
        for b in range(OWN):
            gacc[GR1, b] += mm_t(feat[b, :, chunk_of(c)], dun[c, b])
        return carry

    dun = h1
    lax.fori_loop(0, CHUNKS, row0, 0)
    scatter(GR1)

    def row0_grad(c, carry):
        for b in range(OWN):
            fgradb[b, :, chunk_of(c)] = (g1[c, b].astype(F32) + mm(right[0, b], dun[c, b])).astype(BF16)
        return carry

    lax.fori_loop(0, CHUNKS, row0_grad, 0)
    pltpu.make_async_copy(fgradb, fgrad_hbm, o_sem.at[5]).start()
    store(GL1)
    wait_all(gmy.at[pl.ds(0, SAMP - 1)], r_recv.at[4])
    gmix_ref[...] = gmy[0] + gmy[1] + gmy[2] + gmy[3]
    gather(GR1)
    store(GR1)

    for a in range(8):
        for c in range(CHUNKS):
            wait_all(sendb.at[a, c, pl.ds(0, PEERS - 1)], a_send.at[a, c])
    wait_all(mixs.at[pl.ds(0, PEERS - 1)], m_send.at[0])
    wait_all(gms.at[pl.ds(0, PEERS - 1)], m_send.at[1])
    for a in range(4):
        wait_all(gsend.at[a, pl.ds(0, SAMP - 1)], r_send.at[a])
        wait_all(ag.at[a, pl.ds(0, SAMP - 1)], g_send.at[a])
        wait_all(ag.at[a], o_sem.at[a])
    wait_all(gmy.at[pl.ds(0, SAMP - 1)], r_send.at[4])
    wait_all(outb, o_sem.at[4])
    wait_all(fgradb, o_sem.at[5])


def local(features, cotangent, right_factor, left_factor, mixing):
    width = features.shape[1]
    samples = width // CHUNKS
    vmem = pl.BlockSpec(memory_space=pltpu.VMEM)
    hbm = pl.BlockSpec(memory_space=pl.ANY)
    acts = jax.ShapeDtypeStruct((OWN, BLOCK, width), BF16)
    grads = jax.ShapeDtypeStruct((LAYERS, OWN, BLOCK, BLOCK), BF16)
    chunked = pltpu.VMEM((CHUNKS, OWN, BLOCK, samples), BF16)
    small = pltpu.VMEM((PEERS, 1, 128), F32)
    output, fgrad, gright, gleft, gmix = pl.pallas_call(
        kernel,
        out_shape=(acts, acts, grads, grads, jax.ShapeDtypeStruct((PEERS, 1, 128), F32)),
        in_specs=[vmem] * 5,
        out_specs=(hbm, hbm, hbm, hbm, vmem),
        scratch_shapes=[
            pltpu.VMEM((8, CHUNKS, PEERS, ROWS, samples), BF16),
            pltpu.VMEM((8, CHUNKS, PEERS, ROWS, samples), BF16),
            pltpu.VMEM((4, BLOCK, BLOCK), BF16),
            pltpu.VMEM((LAYERS, OWN, BLOCK, BLOCK), BF16),
            pltpu.VMEM((LAYERS, OWN, BLOCK, BLOCK), BF16),
            pltpu.VMEM((LAYERS, OWN, BLOCK, BLOCK), BF16),
            chunked,
            chunked,
            pltpu.VMEM((LAYERS, CHUNKS, OWN, BLOCK, samples), BF16),
            chunked,
            pltpu.VMEM((OWN, BLOCK, samples), BF16),
            pltpu.VMEM((OWN, BLOCK, samples), BF16),
            pltpu.VMEM((PEERS, ROWS, samples), BF16),
            pltpu.VMEM((4, PEERS, ROWS, 128), F32),
            pltpu.VMEM((OWN, BLOCK, width), BF16),
            pltpu.VMEM((OWN, BLOCK, width), BF16),
            small,
            small,
            pltpu.VMEM((PEERS, 128), F32),
            small,
            small,
            pltpu.VMEM((SAMP, PEERS, 1, 128), F32),
            pltpu.VMEM((4, OWN, BLOCK, BLOCK), F32),
            pltpu.VMEM((4, OWN, BLOCK, BLOCK), BF16),
            pltpu.VMEM((4, SAMP, BLOCK, BLOCK), BF16),
            pltpu.VMEM((4, SAMP, BLOCK, BLOCK), BF16),
            pltpu.SemaphoreType.DMA((8, CHUNKS)),
            pltpu.SemaphoreType.DMA((8, CHUNKS)),
            pltpu.SemaphoreType.DMA((2,)),
            pltpu.SemaphoreType.DMA((2,)),
            pltpu.SemaphoreType.DMA((5,)),
            pltpu.SemaphoreType.DMA((5,)),
            pltpu.SemaphoreType.DMA((4,)),
            pltpu.SemaphoreType.DMA((4,)),
            pltpu.SemaphoreType.DMA((6,)),
        ],
        compiler_params=pltpu.CompilerParams(
            collective_id=0, has_side_effects=True, vmem_limit_bytes=58 * 1024 * 1024
        ),
    )(
        features.reshape(OWN, BLOCK, width),
        cotangent.reshape(OWN, BLOCK, width),
        right_factor,
        left_factor,
        mixing,
    )
    gmix = gmix.reshape(PEERS, 128)[:, :64].reshape(PEERS, LAYERS, 2, OWN, OWN)
    gmix = gmix.transpose(1, 2, 3, 0, 4).reshape(LAYERS, 2, OWN, BLOCK)
    return (
        output.reshape(OWN * BLOCK, width),
        fgrad.reshape(OWN * BLOCK, width),
        gright.astype(F32),
        gleft.astype(F32),
        gmix,
    )


def solution(mesh):
    specs = (
        P(("chan", "bfly"), "samp"),
        P(("chan", "bfly"), "samp"),
        P(None, ("chan", "bfly"), None, None),
        P(None, ("chan", "bfly"), None, None),
        P(None, None, ("chan", "bfly"), None),
    )
    return jax.shard_map(local, mesh=mesh, in_specs=specs, out_specs=specs, check_vma=False)
```

```python
import functools

import jax
import jax.numpy as jnp
from jax import lax
from jax.experimental import pallas as pl
from jax.experimental.pallas import tpu as pltpu
from jax.sharding import PartitionSpec as P

BLOCK = 256
LAYERS = 2
PEERS = 64
OWN = 4
ROWS = 16
GROUPS = 4
GPEERS = PEERS // GROUPS
SAMP = 4
CHUNKS = 2
EARLY = 40
LATE = 17
SPLIT = 33
FINAL = 4
MESH = pl.DeviceIdType.MESH
F32 = jnp.float32
BF16 = jnp.bfloat16

U1, T1, U2, COT, T2, DU2, E1, DU1 = range(8)
GL2, GR2, GL1, GR1 = range(4)
Q_ROW, Q_ROW_T, Q_COL, Q_COL_T = range(4)


def mm(a, b):
    return lax.dot_general(a, b, (((1,), (0,)), ((), ())), preferred_element_type=F32)


def mm_t(a, b):
    return lax.dot_general(a, b, (((1,), (1,)), ((), ())), preferred_element_type=F32)


def flip(groups):
    parts = []
    for pair in range(GPEERS // 2):
        parts += [groups[2 * pair + 1 : 2 * pair + 2], groups[2 * pair : 2 * pair + 1]]
    return jnp.concatenate(parts, axis=0)


def kernel(
    feat_hbm, cot_hbm, right_hbm, left_hbm, mixing,
    out_hbm, fgrad_hbm, gright_hbm, gleft_hbm, gmix_ref,
    feat, cot, right, left, sendb, recvb, qmat, rt, lb, lt, h1, h1d, t1, vn, g1, nat, nat2, dvp, coef, outb, fgradb,
    mixs, mixr, gmacc, gms, gm1, gmy, gacc, gsend, rsr, ag,
    a_send, a_recv, m_send, m_recv, r_send, r_recv, g_send, g_recv, o_sem, i_sem,
):
    samples = h1.shape[3]
    me = lax.axis_index("chan") * 2 + lax.axis_index("bfly")
    y = lax.axis_index("samp")

    def fetch(n, src, dst):
        return pltpu.make_async_copy(src, dst, i_sem.at[n])

    fetches = [
        fetch(0, right_hbm.at[0], right.at[0]),
        fetch(1, feat_hbm, feat),
        fetch(2, cot_hbm, cot),
        fetch(3, left_hbm.at[0], left.at[0]),
        fetch(4, right_hbm.at[1], right.at[1]),
        fetch(5, left_hbm.at[1], left.at[1]),
    ]
    for one_fetch in fetches:
        one_fetch.start()

    def peer_id(p):
        return {"chan": p // 2, "bfly": lax.rem(p, 2)}

    barrier = pltpu.get_barrier_semaphore()

    def greet(k, carry):
        pl.semaphore_signal(barrier, inc=1, device_id=peer_id(lax.rem(me + k, PEERS)), device_id_type=MESH)
        return carry

    lax.fori_loop(1, PEERS, greet, 0)
    for d in range(1, SAMP):
        pl.semaphore_signal(barrier, inc=1, device_id={"samp": lax.rem(y + d, SAMP)}, device_id_type=MESH)

    i0 = lax.broadcasted_iota(jnp.int32, (BLOCK, BLOCK), 0)
    i1 = lax.broadcasted_iota(jnp.int32, (BLOCK, BLOCK), 1)

    def row_of(m):
        return ((m >> 2) & 3) * 64 + (m >> 4) * 4 + (m & 3)

    def col_of(m):
        return (m & 3) * 64 + (m >> 4) * 4 + ((m >> 2) & 3)

    def onehot(mask):
        return jnp.where(mask, 1.0, 0.0).astype(BF16)

    qmat[Q_ROW] = onehot(i1 == row_of(i0))

    def to_peers(which, src, put):
        for g in range(GROUPS):
            x = jnp.concatenate([src[b, 64 * g : 64 * g + 64, :] for b in range(OWN)], axis=0)
            put(g, mm(qmat[which], x))

    def put_into(dst):
        def put(g, value):
            dst[GPEERS * g : GPEERS * (g + 1)] = value.astype(BF16).reshape(GPEERS, ROWS, samples)

        return put

    def split_into(dst, g, value):
        value = value.astype(BF16)
        for b in range(OWN):
            dst[b, 64 * g : 64 * g + 64, :] = value[64 * b : 64 * b + 64]

    def from_peers(which, src, dst):
        for g in range(GROUPS):
            x = src[GPEERS * g : GPEERS * (g + 1)].reshape(BLOCK, samples)
            split_into(dst, g, mm(qmat[which], x))

    def chunk_of(c):
        return pl.ds(pl.multiple_of(c * samples, samples), samples)

    def send(a, c, low=1, high=PEERS):
        def one(k, carry):
            p = lax.rem(me + k, PEERS)
            pltpu.make_async_remote_copy(
                src_ref=sendb.at[a, c, p], dst_ref=recvb.at[a, c, me],
                send_sem=a_send.at[a, c], recv_sem=a_recv.at[a, c],
                device_id=peer_id(p), device_id_type=MESH,
            ).start()
            return carry

        lax.fori_loop(low, high, one, 0)
        if low == 1:
            recvb[a, c, pl.ds(me, 1)] = sendb[a, c, pl.ds(me, 1)]

    def wait_all(ref, sem):
        pltpu.make_async_copy(ref, ref, sem).wait()

    def wait_recv(a, c):
        wait_all(recvb.at[a, c, pl.ds(0, PEERS - 1)], a_recv.at[a, c])

    def first(c):
        for b in range(OWN):
            nat[b] = mm(rt[0, b], feat[b, :, chunk_of(c)]).astype(BF16)
        to_peers(Q_ROW, nat, put_into(sendb.at[U1, c]))

    fetches[0].wait()
    for b in range(OWN):
        rt[0, b] = right[0, b].T
    fetches[1].wait()
    first(0)

    pl.semaphore_wait(barrier, PEERS - 1 + SAMP - 1)

    send(U1, 0)

    pick = onehot((lax.broadcasted_iota(jnp.int32, (BLOCK, 128), 0) & 3) == (lax.broadcasted_iota(jnp.int32, (BLOCK, 128), 1) & 3)).astype(F32)
    lane = lax.broadcasted_iota(jnp.int32, (PEERS, 128), 1)
    owner = lax.broadcasted_iota(jnp.int32, (PEERS, BLOCK), 0)
    unit = lax.broadcasted_iota(jnp.int32, (PEERS, BLOCK), 1)
    message = jnp.zeros((PEERS, 128), F32)
    for r in range(ROWS):
        row = mixing[r // 8, (r // 4) % 2, r % 4 : r % 4 + 1, :]
        spread = jnp.where((unit >> 2) == owner, jnp.broadcast_to(row, (PEERS, BLOCK)), 0.0)
        found = lax.dot_general(
            spread, pick, (((1,), (0,)), ((), ())), precision=lax.Precision.HIGHEST, preferred_element_type=F32
        )
        message = message + jnp.where((lane >> 2) == r, found, 0.0)
    mixs[...] = message.reshape(PEERS, 1, 128)

    def send_mix(k, carry):
        p = lax.rem(me + k, PEERS)
        pltpu.make_async_remote_copy(
            src_ref=mixs.at[p], dst_ref=mixr.at[me], send_sem=m_send.at[0], recv_sem=m_recv.at[0],
            device_id=peer_id(p), device_id_type=MESH,
        ).start()
        return carry

    lax.fori_loop(1, PEERS, send_mix, 0)
    mixr[pl.ds(me, 1)] = mixs[pl.ds(me, 1)]
    for c in range(1, CHUNKS):
        first(c)
        send(U1, c)

    qmat[Q_ROW_T] = onehot(i0 == row_of(i1))
    qmat[Q_COL] = onehot(i1 == col_of(i0))
    qmat[Q_COL_T] = onehot(i0 == col_of(i1))
    fetches[2].wait()
    for c in range(CHUNKS):
        for b in range(OWN):
            nat[b] = cot[b, :, chunk_of(c)]
        to_peers(Q_ROW, nat, put_into(sendb.at[COT, c]))
    for n in (3, 4, 5):
        fetches[n].wait()
    for b in range(OWN):
        rt[1, b] = right[1, b].T
        for layer in range(LAYERS):
            lb[layer, b] = left[layer, b].astype(BF16)
            lt[layer, b] = left[layer, b].T.astype(BF16)
    for a in range(4):
        gacc[a] = jnp.zeros((OWN, BLOCK, BLOCK), F32)
    gmacc[...] = jnp.zeros((PEERS, 128), F32)
    wait_all(mixr.at[pl.ds(0, PEERS - 1)], m_recv.at[0])
    lane3 = lax.broadcasted_iota(jnp.int32, (GPEERS, ROWS, 128), 2)
    row3 = lax.broadcasted_iota(jnp.int32, (GPEERS, ROWS, 128), 1)
    for g in range(GROUPS):
        got = jnp.broadcast_to(mixr[GPEERS * g : GPEERS * (g + 1)], (GPEERS, ROWS, 128))
        for term in range(4):
            value = jnp.sum(jnp.where(lane3 == row3 + ROWS * term, got, 0.0), axis=2, keepdims=True)
            coef[term, GPEERS * g : GPEERS * (g + 1)] = jnp.broadcast_to(value, (GPEERS, ROWS, 128))

    def gain(term, g):
        value = coef[term, GPEERS * g : GPEERS * (g + 1)]
        return jnp.concatenate([value] * (samples // 128), axis=2)

    def mix_forward(layer, a, c):
        for g in range(GROUPS):
            u = recvb[a, c, GPEERS * g : GPEERS * (g + 1)].astype(F32)
            v = (gain(2 * layer, g) * u + gain(2 * layer + 1, g) * flip(u)).astype(BF16)
            split_into(vn.at[layer, c], g, mm(qmat[Q_COL_T], v.reshape(BLOCK, samples)))

    def mix_backward(layer, a, c):
        def put(g, value):
            dv = value.reshape(GPEERS, ROWS, samples)
            dvp[GPEERS * g : GPEERS * (g + 1)] = dv.astype(BF16)
            part = (gain(2 * layer + 1, g) * dv).astype(BF16).astype(F32)
            du = gain(2 * layer, g) * dv + flip(part)
            sendb[a, c, GPEERS * g : GPEERS * (g + 1)] = du.astype(BF16)

        to_peers(Q_COL, nat2, put)

    def mix_gradient(layer, a, c):
        for g in range(GROUPS):
            dv = dvp[GPEERS * g : GPEERS * (g + 1)].astype(F32)
            u = recvb[a, c, GPEERS * g : GPEERS * (g + 1)].astype(F32)
            total = jnp.zeros((GPEERS, ROWS, 128), F32)
            for term, other in ((0, u), (1, flip(u))):
                prod = dv * other
                half = prod[:, :, :128]
                for piece in range(1, samples // 128):
                    half = half + prod[:, :, 128 * piece : 128 * (piece + 1)]
                value = jnp.sum(half, axis=2, keepdims=True)
                total = total + jnp.where(
                    lane3 == row3 + ROWS * (2 * layer + term), jnp.broadcast_to(value, (GPEERS, ROWS, 128)), 0.0
                )
            gmacc[GPEERS * g : GPEERS * (g + 1)] += jnp.sum(total, axis=1)

    def scatter(a):
        gsend[a] = gacc[a].astype(BF16)
        for d in range(1, SAMP):
            to = lax.rem(y + d, SAMP)
            pltpu.make_async_remote_copy(
                src_ref=gsend.at[a, to], dst_ref=rsr.at[a, y], send_sem=r_send.at[a], recv_sem=r_recv.at[a],
                device_id={"samp": to}, device_id_type=MESH,
            ).start()

    def gather(a):
        wait_all(rsr.at[a, pl.ds(0, SAMP - 1)], r_recv.at[a])
        total = gacc[a, y]
        for d in range(1, SAMP):
            total = total + rsr[a, lax.rem(y + d, SAMP)].astype(F32)
        ag[a, y] = total.astype(BF16)
        for d in range(1, SAMP):
            to = lax.rem(y + d, SAMP)
            pltpu.make_async_remote_copy(
                src_ref=ag.at[a, y], dst_ref=ag.at[a, y], send_sem=g_send.at[a], recv_sem=g_recv.at[a],
                device_id={"samp": to}, device_id_type=MESH,
            ).start()

    def store(a):
        wait_all(ag.at[a, pl.ds(0, SAMP - 1)], g_recv.at[a])
        dst = (gleft_hbm if a in (GL1, GL2) else gright_hbm).at[0 if a in (GL1, GR1) else 1]
        pltpu.make_async_copy(ag.at[a], dst, o_sem.at[a]).start()

    def col1(c, carry):
        wait_recv(U1, c)
        mix_forward(0, U1, c)
        for j in range(OWN):
            nat[j] = mm(lt[0, j], vn[0, c, j]).astype(BF16)
        to_peers(Q_COL, nat, put_into(sendb.at[T1, c]))
        send(T1, c)
        send(COT, c)
        return carry

    lax.fori_loop(0, CHUNKS, col1, 0)

    def row2(c, carry):
        wait_recv(T1, c)
        from_peers(Q_ROW_T, recvb.at[T1, c], t1.at[c])
        for b in range(OWN):
            t = t1[c, b].astype(F32)
            h = (feat[b, :, chunk_of(c)].astype(F32) + t * jax.nn.sigmoid(t)).astype(BF16)
            h1[c, b] = h
            nat[b] = mm(rt[1, b], h).astype(BF16)
        to_peers(Q_ROW, nat, put_into(sendb.at[U2, c]))
        send(U2, c)
        return carry

    lax.fori_loop(0, CHUNKS, row2, 0)

    def slope(g, t):
        s = jax.nn.sigmoid(t)
        return (g * s * (1.0 + t * (1.0 - s))).astype(BF16)

    def col2(c, carry):
        wait_recv(COT, c)
        from_peers(Q_COL_T, recvb.at[COT, c], nat2)
        wait_recv(U2, c)
        mix_forward(1, U2, c)
        for j in range(OWN):
            t = mm(lt[1, j], vn[1, c, j]).astype(BF16)
            nat[j] = t
            e = slope(nat2[j].astype(F32), t.astype(F32))
            gacc[GL2, j] += mm_t(vn[1, c, j], e)
            nat2[j] = mm(lb[1, j], e).astype(BF16)
        mix_backward(1, DU2, c)
        send(DU2, c)
        to_peers(Q_COL, nat, put_into(sendb.at[T2, c]))
        mix_gradient(1, U2, c)
        return carry

    lax.fori_loop(0, CHUNKS, col2, 0)
    scatter(GL2)
    send(T2, 0, 1, EARLY)

    def row1(c, carry):
        wait_recv(DU2, c)
        from_peers(Q_ROW_T, recvb.at[DU2, c], nat)
        for b in range(OWN):
            g = (cot[b, :, chunk_of(c)].astype(F32) + mm(right[1, b], nat[b])).astype(BF16)
            g1[c, b] = g
            nat2[b] = slope(g.astype(F32), t1[c, b].astype(F32))
        to_peers(Q_ROW, nat2, put_into(sendb.at[E1, c]))
        send(E1, c)
        for b in range(OWN):
            gacc[GR2, b] += mm_t(h1[c, b], nat[b])
        return carry

    lax.fori_loop(0, CHUNKS, row1, 0)
    gather(GL2)
    scatter(GR2)

    def col1_back(c):
        wait_recv(E1, c)
        from_peers(Q_COL_T, recvb.at[E1, c], nat)
        for j in range(OWN):
            nat2[j] = mm(lb[0, j], nat[j]).astype(BF16)
        mix_backward(0, DU1, c)

    def col1_grad(c):
        for j in range(OWN):
            gacc[GL1, j] += mm_t(vn[0, c, j], nat[j])

    col1_back(0)
    send(DU1, 0)
    col1_grad(0)
    mix_gradient(0, U1, 0)
    gather(GR2)
    store(GL2)
    col1_back(1)
    col1_grad(1)
    scatter(GL1)
    send(DU1, 1, 1, SPLIT)
    mix_gradient(0, U1, 1)
    gms[...] = gmacc[...].reshape(PEERS, 1, 128)

    def send_gm(k, carry):
        p = lax.rem(me + k, PEERS)
        pltpu.make_async_remote_copy(
            src_ref=gms.at[p], dst_ref=gm1.at[me], send_sem=m_send.at[1], recv_sem=m_recv.at[1],
            device_id=peer_id(p), device_id_type=MESH,
        ).start()
        return carry

    lax.fori_loop(1, PEERS, send_gm, 0)
    gm1[pl.ds(me, 1)] = gms[pl.ds(me, 1)]
    gather(GL1)
    send(DU1, 1, SPLIT, PEERS)
    store(GR2)

    dun = h1d

    def row0(c, carry):
        wait_recv(DU1, c)
        from_peers(Q_ROW_T, recvb.at[DU1, c], dun.at[c])
        for b in range(OWN):
            gacc[GR1, b] += mm_t(feat[b, :, chunk_of(c)], dun[c, b])
        return carry

    lax.fori_loop(0, CHUNKS, row0, 0)
    scatter(GR1)
    wait_all(gm1.at[pl.ds(0, PEERS - 1)], m_recv.at[1])
    gmy[pl.ds(y, 1)] = gm1[...].reshape(1, PEERS, 1, 128)
    for d in range(1, SAMP):
        to = lax.rem(y + d, SAMP)
        pltpu.make_async_remote_copy(
            src_ref=gm1, dst_ref=gmy.at[y], send_sem=r_send.at[4], recv_sem=r_recv.at[4],
            device_id={"samp": to}, device_id_type=MESH,
        ).start()
    if EARLY < PEERS:
        send(T2, 0, EARLY, PEERS)
    send(T2, 1, 1, LATE)

    def row0_grad(c, carry):
        for b in range(OWN):
            fgradb[b, :, chunk_of(c)] = (g1[c, b].astype(F32) + mm(right[0, b], dun[c, b])).astype(BF16)
        return carry

    lax.fori_loop(0, CHUNKS, row0_grad, 0)
    pltpu.make_async_copy(fgradb, fgrad_hbm, o_sem.at[5]).start()
    store(GL1)
    gather(GR1)
    send(T2, 1, LATE, PEERS)
    wait_all(gmy.at[pl.ds(0, SAMP - 1)], r_recv.at[4])
    total = (gmy[0] + gmy[1] + gmy[2] + gmy[3]).reshape(PEERS, 128)
    spread_back = onehot(
        (lax.broadcasted_iota(jnp.int32, (128, BLOCK), 0) & 3) == (lax.broadcasted_iota(jnp.int32, (128, BLOCK), 1) & 3)
    ).astype(F32)
    for r in range(ROWS):
        found = lax.dot_general(
            jnp.where((lane >> 2) == r, total, 0.0), spread_back, (((1,), (0,)), ((), ())),
            precision=lax.Precision.HIGHEST, preferred_element_type=F32,
        )
        gmix_ref[r // 8, (r // 4) % 2, r % 4 : r % 4 + 1, :] = jnp.sum(
            jnp.where((unit >> 2) == owner, found, 0.0), axis=0, keepdims=True
        )

    def final_output(c, carry):
        wait_recv(T2, c)
        from_peers(Q_ROW_T, recvb.at[T2, c], nat)
        for b in range(OWN):
            t = nat[b].astype(F32)
            outb[b, :, chunk_of(c)] = (h1[c, b].astype(F32) + t * jax.nn.sigmoid(t)).astype(BF16)
        return carry

    lax.fori_loop(0, CHUNKS, final_output, 0)
    pltpu.make_async_copy(outb, out_hbm, o_sem.at[4]).start()
    store(GR1)

    for a in range(8):
        for c in range(CHUNKS):
            wait_all(sendb.at[a, c, pl.ds(0, PEERS - 1)], a_send.at[a, c])
    wait_all(mixs.at[pl.ds(0, PEERS - 1)], m_send.at[0])
    wait_all(gms.at[pl.ds(0, PEERS - 1)], m_send.at[1])
    for a in range(4):
        wait_all(gsend.at[a, pl.ds(0, SAMP - 1)], r_send.at[a])
        wait_all(ag.at[a, pl.ds(0, SAMP - 1)], g_send.at[a])
        wait_all(ag.at[a], o_sem.at[a])
    wait_all(gmy.at[pl.ds(0, SAMP - 1)], r_send.at[4])
    wait_all(outb, o_sem.at[4])
    wait_all(fgradb, o_sem.at[5])


def finish(out_in, fgrad_in, gright_in, gleft_in, gmix_in, out, fgrad, gright, gleft, gmix):
    out[...] = out_in[...]
    fgrad[...] = fgrad_in[...]
    gright[...] = gright_in[...].astype(F32)
    gleft[...] = gleft_in[...].astype(F32)
    gmix[...] = gmix_in[...]


def local(features, cotangent, right_factor, left_factor, mixing):
    width = features.shape[1]
    samples = width // CHUNKS
    vmem = pl.BlockSpec(memory_space=pltpu.VMEM)
    hbm = pl.BlockSpec(memory_space=pl.ANY)
    acts = jax.ShapeDtypeStruct((OWN, BLOCK, width), BF16)
    grads = jax.ShapeDtypeStruct((LAYERS, OWN, BLOCK, BLOCK), BF16)
    chunked = pltpu.VMEM((CHUNKS, OWN, BLOCK, samples), BF16)
    small = pltpu.VMEM((PEERS, 1, 128), F32)
    output, fgrad, gright, gleft, gmix = pl.pallas_call(
        kernel,
        out_shape=(acts, acts, grads, grads, jax.ShapeDtypeStruct((LAYERS, 2, OWN, BLOCK), F32)),
        in_specs=[hbm] * 4 + [vmem],
        out_specs=(hbm, hbm, hbm, hbm, vmem),
        scratch_shapes=[
            pltpu.VMEM((OWN, BLOCK, width), BF16),
            pltpu.VMEM((OWN, BLOCK, width), BF16),
            pltpu.VMEM((LAYERS, OWN, BLOCK, BLOCK), BF16),
            pltpu.VMEM((LAYERS, OWN, BLOCK, BLOCK), F32),
            pltpu.VMEM((8, CHUNKS, PEERS, ROWS, samples), BF16),
            pltpu.VMEM((8, CHUNKS, PEERS, ROWS, samples), BF16),
            pltpu.VMEM((4, BLOCK, BLOCK), BF16),
            pltpu.VMEM((LAYERS, OWN, BLOCK, BLOCK), BF16),
            pltpu.VMEM((LAYERS, OWN, BLOCK, BLOCK), BF16),
            pltpu.VMEM((LAYERS, OWN, BLOCK, BLOCK), BF16),
            chunked,
            chunked,
            chunked,
            pltpu.VMEM((LAYERS, CHUNKS, OWN, BLOCK, samples), BF16),
            chunked,
            pltpu.VMEM((OWN, BLOCK, samples), BF16),
            pltpu.VMEM((OWN, BLOCK, samples), BF16),
            pltpu.VMEM((PEERS, ROWS, samples), BF16),
            pltpu.VMEM((4, PEERS, ROWS, 128), F32),
            pltpu.VMEM((OWN, BLOCK, width), BF16),
            pltpu.VMEM((OWN, BLOCK, width), BF16),
            small,
            small,
            pltpu.VMEM((PEERS, 128), F32),
            small,
            small,
            pltpu.VMEM((SAMP, PEERS, 1, 128), F32),
            pltpu.VMEM((4, OWN, BLOCK, BLOCK), F32),
            pltpu.VMEM((4, OWN, BLOCK, BLOCK), BF16),
            pltpu.VMEM((4, SAMP, BLOCK, BLOCK), BF16),
            pltpu.VMEM((4, SAMP, BLOCK, BLOCK), BF16),
            pltpu.SemaphoreType.DMA((8, CHUNKS)),
            pltpu.SemaphoreType.DMA((8, CHUNKS)),
            pltpu.SemaphoreType.DMA((2,)),
            pltpu.SemaphoreType.DMA((2,)),
            pltpu.SemaphoreType.DMA((5,)),
            pltpu.SemaphoreType.DMA((5,)),
            pltpu.SemaphoreType.DMA((4,)),
            pltpu.SemaphoreType.DMA((4,)),
            pltpu.SemaphoreType.DMA((6,)),
            pltpu.SemaphoreType.DMA((6,)),
        ],
        compiler_params=pltpu.CompilerParams(
            collective_id=0, has_side_effects=True, vmem_limit_bytes=58 * 1024 * 1024
        ),
    )(
        features.reshape(OWN, BLOCK, width),
        cotangent.reshape(OWN, BLOCK, width),
        right_factor,
        left_factor,
        mixing,
    )
    rows = OWN * BLOCK
    step = rows // FINAL
    blocks = LAYERS * OWN // FINAL
    wide = pl.BlockSpec((step, width), lambda i: (i, 0))
    block = pl.BlockSpec((blocks, BLOCK, BLOCK), lambda i: (i, 0, 0))
    whole = pl.BlockSpec((LAYERS, 2, OWN, BLOCK), lambda i: (0, 0, 0, 0))
    flat = (LAYERS * OWN, BLOCK, BLOCK)
    output, fgrad, gright, gleft, gmix = pl.pallas_call(
        finish,
        grid=(FINAL,),
        out_shape=(
            jax.ShapeDtypeStruct((rows, width), BF16),
            jax.ShapeDtypeStruct((rows, width), BF16),
            jax.ShapeDtypeStruct(flat, F32),
            jax.ShapeDtypeStruct(flat, F32),
            jax.ShapeDtypeStruct((LAYERS, 2, OWN, BLOCK), F32),
        ),
        in_specs=[wide, wide, block, block, whole],
        out_specs=(wide, wide, block, block, whole),
    )(output.reshape(rows, width), fgrad.reshape(rows, width), gright.reshape(flat), gleft.reshape(flat), gmix)
    shape = (LAYERS, OWN, BLOCK, BLOCK)
    return output, fgrad, gright.reshape(shape), gleft.reshape(shape), gmix


def solution(mesh):
    specs = (
        P(("chan", "bfly"), "samp"),
        P(("chan", "bfly"), "samp"),
        P(None, ("chan", "bfly"), None, None),
        P(None, ("chan", "bfly"), None, None),
        P(None, None, ("chan", "bfly"), None),
    )
    return jax.shard_map(local, mesh=mesh, in_specs=specs, out_specs=specs, check_vma=False)
```

```python
import functools

import jax
import jax.numpy as jnp
from jax import lax
from jax.experimental import pallas as pl
from jax.experimental.pallas import tpu as pltpu
from jax.sharding import PartitionSpec as P

BLOCK = 256
LAYERS = 2
PEERS = 64
OWN = 4
ROWS = 16
GROUPS = 4
GPEERS = PEERS // GROUPS
SAMP = 4
CHUNKS = 2
EARLY = 40
LATE = 17
SPLIT = 33
MESH = pl.DeviceIdType.MESH
F32 = jnp.float32
BF16 = jnp.bfloat16

U1, T1, U2, COT, T2, DU2, E1, DU1 = range(8)
GL2, GR2, GL1, GR1 = range(4)
Q_ROW, Q_ROW_T, Q_COL, Q_COL_T = range(4)


def mm(a, b):
    return lax.dot_general(a, b, (((1,), (0,)), ((), ())), preferred_element_type=F32)


def mm_t(a, b):
    return lax.dot_general(a, b, (((1,), (1,)), ((), ())), preferred_element_type=F32)


def flip(groups):
    parts = []
    for pair in range(GPEERS // 2):
        parts += [groups[2 * pair + 1 : 2 * pair + 2], groups[2 * pair : 2 * pair + 1]]
    return jnp.concatenate(parts, axis=0)


def kernel(
    feat_hbm, cot_hbm, right_hbm, left_hbm, mixing_hbm,
    out_hbm, fgrad_hbm, gright_hbm, gleft_hbm, gmix_ref,
    feat, cot, right, left, mixing, sendb, recvb, qmat, rt, lb, lt, h1, h1d, t1, vn, g1, nat, nat2, dvp, coef, outb, fgradb,
    mixs, mixr, gmacc, gms, gm1, gmy, gacc, gsend, rsr, ag,
    a_send, a_recv, m_send, m_recv, r_send, r_recv, g_send, g_recv, o_sem, i_sem,
):
    samples = h1.shape[3]
    me = lax.axis_index("chan") * 2 + lax.axis_index("bfly")
    y = lax.axis_index("samp")

    def fetch(n, src, dst):
        return pltpu.make_async_copy(src, dst, i_sem.at[n])

    fetches = [
        fetch(2, cot_hbm, cot),
        fetch(0, right_hbm.at[0], right.at[0]),
        fetch(1, feat_hbm, feat),
        fetch(3, left_hbm.at[0], left.at[0]),
        fetch(4, right_hbm.at[1], right.at[1]),
        fetch(5, left_hbm.at[1], left.at[1]),
        fetch(6, mixing_hbm, mixing),
    ]
    for one_fetch in fetches:
        one_fetch.start()
    fetches = [fetches[1], fetches[2], fetches[0]] + fetches[3:]

    def peer_id(p):
        return {"chan": p // 2, "bfly": lax.rem(p, 2)}

    barrier = pltpu.get_barrier_semaphore()

    def greet(k, carry):
        pl.semaphore_signal(barrier, inc=1, device_id=peer_id(lax.rem(me + k, PEERS)), device_id_type=MESH)
        return carry

    lax.fori_loop(1, PEERS, greet, 0)
    for d in range(1, SAMP):
        pl.semaphore_signal(barrier, inc=1, device_id={"samp": lax.rem(y + d, SAMP)}, device_id_type=MESH)

    i0 = lax.broadcasted_iota(jnp.int32, (BLOCK, BLOCK), 0)
    i1 = lax.broadcasted_iota(jnp.int32, (BLOCK, BLOCK), 1)

    def row_of(m):
        return ((m >> 2) & 3) * 64 + (m >> 4) * 4 + (m & 3)

    def col_of(m):
        return (m & 3) * 64 + (m >> 4) * 4 + ((m >> 2) & 3)

    def onehot(mask):
        return jnp.where(mask, 1.0, 0.0).astype(BF16)

    qmat[Q_ROW] = onehot(i1 == row_of(i0))

    def to_peers(which, src, put):
        for g in range(GROUPS):
            x = jnp.concatenate([src[b, 64 * g : 64 * g + 64, :] for b in range(OWN)], axis=0)
            put(g, mm(qmat[which], x))

    def put_into(dst):
        def put(g, value):
            dst[GPEERS * g : GPEERS * (g + 1)] = value.astype(BF16).reshape(GPEERS, ROWS, samples)

        return put

    def split_into(dst, g, value):
        value = value.astype(BF16)
        for b in range(OWN):
            dst[b, 64 * g : 64 * g + 64, :] = value[64 * b : 64 * b + 64]

    def from_peers(which, src, dst):
        for g in range(GROUPS):
            x = src[GPEERS * g : GPEERS * (g + 1)].reshape(BLOCK, samples)
            split_into(dst, g, mm(qmat[which], x))

    def chunk_of(c):
        return pl.ds(pl.multiple_of(c * samples, samples), samples)

    def send(a, c, low=1, high=PEERS):
        def one(k, carry):
            p = lax.rem(me + k, PEERS)
            pltpu.make_async_remote_copy(
                src_ref=sendb.at[a, c, p], dst_ref=recvb.at[a, c, me],
                send_sem=a_send.at[a, c], recv_sem=a_recv.at[a, c],
                device_id=peer_id(p), device_id_type=MESH,
            ).start()
            return carry

        lax.fori_loop(low, high, one, 0)
        if low == 1:
            recvb[a, c, pl.ds(me, 1)] = sendb[a, c, pl.ds(me, 1)]

    def wait_all(ref, sem):
        pltpu.make_async_copy(ref, ref, sem).wait()

    def wait_recv(a, c):
        wait_all(recvb.at[a, c, pl.ds(0, PEERS - 1)], a_recv.at[a, c])

    def first(c):
        for b in range(OWN):
            nat[b] = mm(rt[0, b], feat[b, :, chunk_of(c)]).astype(BF16)
        to_peers(Q_ROW, nat, put_into(sendb.at[U1, c]))

    def first_cot(c):
        for b in range(OWN):
            nat2[b] = cot[b, :, chunk_of(c)]
        to_peers(Q_ROW, nat2, put_into(sendb.at[COT, c]))

    fetches[2].wait()
    first_cot(0)
    pl.semaphore_wait(barrier, PEERS - 1 + SAMP - 1)
    send(COT, 0)
    fetches[0].wait()
    for b in range(OWN):
        rt[0, b] = right[0, b].T
    fetches[1].wait()
    first(0)
    send(U1, 0)

    pick = onehot((lax.broadcasted_iota(jnp.int32, (BLOCK, 128), 0) & 3) == (lax.broadcasted_iota(jnp.int32, (BLOCK, 128), 1) & 3)).astype(F32)
    lane = lax.broadcasted_iota(jnp.int32, (PEERS, 128), 1)
    owner = lax.broadcasted_iota(jnp.int32, (PEERS, BLOCK), 0)
    unit = lax.broadcasted_iota(jnp.int32, (PEERS, BLOCK), 1)
    fetches[6].wait()
    message = jnp.zeros((PEERS, 128), F32)
    for r in range(ROWS):
        row = mixing[r // 8, (r // 4) % 2, r % 4 : r % 4 + 1, :]
        spread = jnp.where((unit >> 2) == owner, jnp.broadcast_to(row, (PEERS, BLOCK)), 0.0)
        found = lax.dot_general(
            spread, pick, (((1,), (0,)), ((), ())), precision=lax.Precision.HIGHEST, preferred_element_type=F32
        )
        message = message + jnp.where((lane >> 2) == r, found, 0.0)
    mixs[...] = message.reshape(PEERS, 1, 128)

    def send_mix(k, carry):
        p = lax.rem(me + k, PEERS)
        pltpu.make_async_remote_copy(
            src_ref=mixs.at[p], dst_ref=mixr.at[me], send_sem=m_send.at[0], recv_sem=m_recv.at[0],
            device_id=peer_id(p), device_id_type=MESH,
        ).start()
        return carry

    lax.fori_loop(1, PEERS, send_mix, 0)
    mixr[pl.ds(me, 1)] = mixs[pl.ds(me, 1)]
    for c in range(1, CHUNKS):
        first(c)
        send(U1, c)

    qmat[Q_ROW_T] = onehot(i0 == row_of(i1))
    qmat[Q_COL] = onehot(i1 == col_of(i0))
    qmat[Q_COL_T] = onehot(i0 == col_of(i1))
    for c in range(1, CHUNKS):
        first_cot(c)
    for n in (3, 4, 5):
        fetches[n].wait()
    for b in range(OWN):
        rt[1, b] = right[1, b].T
        for layer in range(LAYERS):
            lb[layer, b] = left[layer, b].astype(BF16)
            lt[layer, b] = left[layer, b].T.astype(BF16)
    for a in range(4):
        gacc[a] = jnp.zeros((OWN, BLOCK, BLOCK), F32)
    gmacc[...] = jnp.zeros((PEERS, 128), F32)
    wait_all(mixr.at[pl.ds(0, PEERS - 1)], m_recv.at[0])
    lane3 = lax.broadcasted_iota(jnp.int32, (GPEERS, ROWS, 128), 2)
    row3 = lax.broadcasted_iota(jnp.int32, (GPEERS, ROWS, 128), 1)
    for g in range(GROUPS):
        got = jnp.broadcast_to(mixr[GPEERS * g : GPEERS * (g + 1)], (GPEERS, ROWS, 128))
        for term in range(4):
            value = jnp.sum(jnp.where(lane3 == row3 + ROWS * term, got, 0.0), axis=2, keepdims=True)
            coef[term, GPEERS * g : GPEERS * (g + 1)] = jnp.broadcast_to(value, (GPEERS, ROWS, 128))

    def gain(term, g):
        value = coef[term, GPEERS * g : GPEERS * (g + 1)]
        return jnp.concatenate([value] * (samples // 128), axis=2)

    def mix_forward(layer, a, c):
        for g in range(GROUPS):
            u = recvb[a, c, GPEERS * g : GPEERS * (g + 1)].astype(F32)
            v = (gain(2 * layer, g) * u + gain(2 * layer + 1, g) * flip(u)).astype(BF16)
            split_into(vn.at[layer, c], g, mm(qmat[Q_COL_T], v.reshape(BLOCK, samples)))

    def mix_backward(layer, a, c):
        def put(g, value):
            dv = value.reshape(GPEERS, ROWS, samples)
            dvp[GPEERS * g : GPEERS * (g + 1)] = dv.astype(BF16)
            part = (gain(2 * layer + 1, g) * dv).astype(BF16).astype(F32)
            du = gain(2 * layer, g) * dv + flip(part)
            sendb[a, c, GPEERS * g : GPEERS * (g + 1)] = du.astype(BF16)

        to_peers(Q_COL, nat2, put)

    def mix_gradient(layer, a, c):
        for g in range(GROUPS):
            dv = dvp[GPEERS * g : GPEERS * (g + 1)].astype(F32)
            u = recvb[a, c, GPEERS * g : GPEERS * (g + 1)].astype(F32)
            total = jnp.zeros((GPEERS, ROWS, 128), F32)
            for term, other in ((0, u), (1, flip(u))):
                prod = dv * other
                half = prod[:, :, :128]
                for piece in range(1, samples // 128):
                    half = half + prod[:, :, 128 * piece : 128 * (piece + 1)]
                value = jnp.sum(half, axis=2, keepdims=True)
                total = total + jnp.where(
                    lane3 == row3 + ROWS * (2 * layer + term), jnp.broadcast_to(value, (GPEERS, ROWS, 128)), 0.0
                )
            gmacc[GPEERS * g : GPEERS * (g + 1)] += jnp.sum(total, axis=1)

    def scatter(a):
        gsend[a] = gacc[a].astype(BF16)
        for d in range(1, SAMP):
            to = lax.rem(y + d, SAMP)
            pltpu.make_async_remote_copy(
                src_ref=gsend.at[a, to], dst_ref=rsr.at[a, y], send_sem=r_send.at[a], recv_sem=r_recv.at[a],
                device_id={"samp": to}, device_id_type=MESH,
            ).start()

    def gather(a):
        wait_all(rsr.at[a, pl.ds(0, SAMP - 1)], r_recv.at[a])
        total = gacc[a, y]
        for d in range(1, SAMP):
            total = total + rsr[a, lax.rem(y + d, SAMP)].astype(F32)
        ag[a, y] = total.astype(BF16)
        for d in range(1, SAMP):
            to = lax.rem(y + d, SAMP)
            pltpu.make_async_remote_copy(
                src_ref=ag.at[a, y], dst_ref=ag.at[a, y], send_sem=g_send.at[a], recv_sem=g_recv.at[a],
                device_id={"samp": to}, device_id_type=MESH,
            ).start()

    def store(a):
        wait_all(ag.at[a, pl.ds(0, SAMP - 1)], g_recv.at[a])
        dst = (gleft_hbm if a in (GL1, GL2) else gright_hbm).at[0 if a in (GL1, GR1) else 1]
        pltpu.make_async_copy(ag.at[a], dst, o_sem.at[a]).start()

    def col1(c, carry):
        wait_recv(U1, c)
        mix_forward(0, U1, c)
        for j in range(OWN):
            nat[j] = mm(lt[0, j], vn[0, c, j]).astype(BF16)
        to_peers(Q_COL, nat, put_into(sendb.at[T1, c]))
        send(T1, c)
        return carry

    lax.fori_loop(0, CHUNKS, col1, 0)
    for c in range(1, CHUNKS):
        send(COT, c)

    def row2(c, carry):
        wait_recv(T1, c)
        from_peers(Q_ROW_T, recvb.at[T1, c], t1.at[c])
        for b in range(OWN):
            t = t1[c, b].astype(F32)
            h = (feat[b, :, chunk_of(c)].astype(F32) + t * jax.nn.sigmoid(t)).astype(BF16)
            h1[c, b] = h
            nat[b] = mm(rt[1, b], h).astype(BF16)
        to_peers(Q_ROW, nat, put_into(sendb.at[U2, c]))
        send(U2, c)
        return carry

    lax.fori_loop(0, CHUNKS, row2, 0)

    def slope(g, t):
        s = jax.nn.sigmoid(t)
        return (g * s * (1.0 + t * (1.0 - s))).astype(BF16)

    def col2(c, carry):
        wait_recv(COT, c)
        from_peers(Q_COL_T, recvb.at[COT, c], nat2)
        wait_recv(U2, c)
        mix_forward(1, U2, c)
        for j in range(OWN):
            t = mm(lt[1, j], vn[1, c, j]).astype(BF16)
            nat[j] = t
            e = slope(nat2[j].astype(F32), t.astype(F32))
            gacc[GL2, j] += mm_t(vn[1, c, j], e)
            nat2[j] = mm(lb[1, j], e).astype(BF16)
        mix_backward(1, DU2, c)
        send(DU2, c)
        to_peers(Q_COL, nat, put_into(sendb.at[T2, c]))
        mix_gradient(1, U2, c)
        return carry

    lax.fori_loop(0, CHUNKS, col2, 0)
    scatter(GL2)
    send(T2, 0, 1, EARLY)

    def row1(c, carry):
        wait_recv(DU2, c)
        from_peers(Q_ROW_T, recvb.at[DU2, c], nat)
        for b in range(OWN):
            g = (cot[b, :, chunk_of(c)].astype(F32) + mm(right[1, b], nat[b])).astype(BF16)
            g1[c, b] = g
            nat2[b] = slope(g.astype(F32), t1[c, b].astype(F32))
        to_peers(Q_ROW, nat2, put_into(sendb.at[E1, c]))
        send(E1, c)
        for b in range(OWN):
            gacc[GR2, b] += mm_t(h1[c, b], nat[b])
        return carry

    lax.fori_loop(0, CHUNKS, row1, 0)
    gather(GL2)
    scatter(GR2)

    def col1_back(c):
        wait_recv(E1, c)
        from_peers(Q_COL_T, recvb.at[E1, c], nat)
        for j in range(OWN):
            nat2[j] = mm(lb[0, j], nat[j]).astype(BF16)
        mix_backward(0, DU1, c)

    def col1_grad(c):
        for j in range(OWN):
            gacc[GL1, j] += mm_t(vn[0, c, j], nat[j])

    col1_back(0)
    send(DU1, 0)
    col1_grad(0)
    mix_gradient(0, U1, 0)
    col1_back(1)
    send(DU1, 1, 1, SPLIT)
    col1_grad(1)
    scatter(GL1)
    mix_gradient(0, U1, 1)
    gather(GR2)
    store(GL2)
    gms[...] = gmacc[...].reshape(PEERS, 1, 128)

    def send_gm(k, carry):
        p = lax.rem(me + k, PEERS)
        pltpu.make_async_remote_copy(
            src_ref=gms.at[p], dst_ref=gm1.at[me], send_sem=m_send.at[1], recv_sem=m_recv.at[1],
            device_id=peer_id(p), device_id_type=MESH,
        ).start()
        return carry

    lax.fori_loop(1, PEERS, send_gm, 0)
    gm1[pl.ds(me, 1)] = gms[pl.ds(me, 1)]
    gather(GL1)
    send(DU1, 1, SPLIT, PEERS)
    store(GR2)

    dun = h1d

    def row0(c, carry):
        wait_recv(DU1, c)
        from_peers(Q_ROW_T, recvb.at[DU1, c], dun.at[c])
        for b in range(OWN):
            gacc[GR1, b] += mm_t(feat[b, :, chunk_of(c)], dun[c, b])
        return carry

    lax.fori_loop(0, CHUNKS, row0, 0)
    scatter(GR1)
    wait_all(gm1.at[pl.ds(0, PEERS - 1)], m_recv.at[1])
    gmy[pl.ds(y, 1)] = gm1[...].reshape(1, PEERS, 1, 128)
    for d in range(1, SAMP):
        to = lax.rem(y + d, SAMP)
        pltpu.make_async_remote_copy(
            src_ref=gm1, dst_ref=gmy.at[y], send_sem=r_send.at[4], recv_sem=r_recv.at[4],
            device_id={"samp": to}, device_id_type=MESH,
        ).start()
    if EARLY < PEERS:
        send(T2, 0, EARLY, PEERS)
    send(T2, 1, 1, LATE)

    def row0_grad(c, carry):
        for b in range(OWN):
            fgradb[b, :, chunk_of(c)] = (g1[c, b].astype(F32) + mm(right[0, b], dun[c, b])).astype(BF16)
        return carry

    lax.fori_loop(0, CHUNKS, row0_grad, 0)
    pltpu.make_async_copy(fgradb, fgrad_hbm, o_sem.at[5]).start()
    store(GL1)
    gather(GR1)
    send(T2, 1, LATE, PEERS)
    wait_all(gmy.at[pl.ds(0, SAMP - 1)], r_recv.at[4])
    total = (gmy[0] + gmy[1] + gmy[2] + gmy[3]).reshape(PEERS, 128)
    spread_back = onehot(
        (lax.broadcasted_iota(jnp.int32, (128, BLOCK), 0) & 3) == (lax.broadcasted_iota(jnp.int32, (128, BLOCK), 1) & 3)
    ).astype(F32)
    for r in range(ROWS):
        found = lax.dot_general(
            jnp.where((lane >> 2) == r, total, 0.0), spread_back, (((1,), (0,)), ((), ())),
            precision=lax.Precision.HIGHEST, preferred_element_type=F32,
        )
        gmix_ref[r // 8, (r // 4) % 2, r % 4 : r % 4 + 1, :] = jnp.sum(
            jnp.where((unit >> 2) == owner, found, 0.0), axis=0, keepdims=True
        )

    def final_output(c, carry):
        wait_recv(T2, c)
        from_peers(Q_ROW_T, recvb.at[T2, c], nat)
        for b in range(OWN):
            t = nat[b].astype(F32)
            outb[b, :, chunk_of(c)] = (h1[c, b].astype(F32) + t * jax.nn.sigmoid(t)).astype(BF16)
        return carry

    lax.fori_loop(0, CHUNKS, final_output, 0)
    pltpu.make_async_copy(outb, out_hbm, o_sem.at[4]).start()
    store(GR1)

    for a in range(8):
        for c in range(CHUNKS):
            wait_all(sendb.at[a, c, pl.ds(0, PEERS - 1)], a_send.at[a, c])
    wait_all(mixs.at[pl.ds(0, PEERS - 1)], m_send.at[0])
    wait_all(gms.at[pl.ds(0, PEERS - 1)], m_send.at[1])
    for a in range(4):
        wait_all(gsend.at[a, pl.ds(0, SAMP - 1)], r_send.at[a])
        wait_all(ag.at[a, pl.ds(0, SAMP - 1)], g_send.at[a])
        wait_all(ag.at[a], o_sem.at[a])
    wait_all(gmy.at[pl.ds(0, SAMP - 1)], r_send.at[4])
    wait_all(outb, o_sem.at[4])
    wait_all(fgradb, o_sem.at[5])


def finish(out_in, fgrad_in, gright_in, gleft_in, gmix_in, out, fgrad, gright, gleft, gmix, wide, sem):
    whole = [
        pltpu.make_async_copy(src, dst, sem.at[0, n])
        for n, (src, dst) in enumerate(((out_in, out), (fgrad_in, fgrad), (gmix_in, gmix)))
    ]
    for copy in whole:
        copy.start()
    pieces = []
    for n, (src, dst) in enumerate(((gright_in, gright), (gleft_in, gleft))):
        for layer in range(LAYERS):
            for b in range(OWN):
                wide[n, layer, b] = src[layer, b].astype(F32)
                copy = pltpu.make_async_copy(wide.at[n, layer, b], dst.at[layer, b], sem.at[1 + n, OWN * layer + b])
                copy.start()
                pieces.append(copy)
    for copy in whole + pieces:
        copy.wait()


def local(features, cotangent, right_factor, left_factor, mixing):
    width = features.shape[1]
    samples = width // CHUNKS
    vmem = pl.BlockSpec(memory_space=pltpu.VMEM)
    hbm = pl.BlockSpec(memory_space=pl.ANY)
    acts = jax.ShapeDtypeStruct((OWN, BLOCK, width), BF16)
    grads = jax.ShapeDtypeStruct((LAYERS, OWN, BLOCK, BLOCK), BF16)
    chunked = pltpu.VMEM((CHUNKS, OWN, BLOCK, samples), BF16)
    small = pltpu.VMEM((PEERS, 1, 128), F32)
    output, fgrad, gright, gleft, gmix = pl.pallas_call(
        kernel,
        out_shape=(acts, acts, grads, grads, jax.ShapeDtypeStruct((LAYERS, 2, OWN, BLOCK), F32)),
        in_specs=[pl.BlockSpec(memory_space=pltpu.HBM)] * 5,
        out_specs=(hbm, hbm, hbm, hbm, vmem),
        scratch_shapes=[
            pltpu.VMEM((OWN, BLOCK, width), BF16),
            pltpu.VMEM((OWN, BLOCK, width), BF16),
            pltpu.VMEM((LAYERS, OWN, BLOCK, BLOCK), BF16),
            pltpu.VMEM((LAYERS, OWN, BLOCK, BLOCK), F32),
            pltpu.VMEM((LAYERS, 2, OWN, BLOCK), F32),
            pltpu.VMEM((8, CHUNKS, PEERS, ROWS, samples), BF16),
            pltpu.VMEM((8, CHUNKS, PEERS, ROWS, samples), BF16),
            pltpu.VMEM((4, BLOCK, BLOCK), BF16),
            pltpu.VMEM((LAYERS, OWN, BLOCK, BLOCK), BF16),
            pltpu.VMEM((LAYERS, OWN, BLOCK, BLOCK), BF16),
            pltpu.VMEM((LAYERS, OWN, BLOCK, BLOCK), BF16),
            chunked,
            chunked,
            chunked,
            pltpu.VMEM((LAYERS, CHUNKS, OWN, BLOCK, samples), BF16),
            chunked,
            pltpu.VMEM((OWN, BLOCK, samples), BF16),
            pltpu.VMEM((OWN, BLOCK, samples), BF16),
            pltpu.VMEM((PEERS, ROWS, samples), BF16),
            pltpu.VMEM((4, PEERS, ROWS, 128), F32),
            pltpu.VMEM((OWN, BLOCK, width), BF16),
            pltpu.VMEM((OWN, BLOCK, width), BF16),
            small,
            small,
            pltpu.VMEM((PEERS, 128), F32),
            small,
            small,
            pltpu.VMEM((SAMP, PEERS, 1, 128), F32),
            pltpu.VMEM((4, OWN, BLOCK, BLOCK), F32),
            pltpu.VMEM((4, OWN, BLOCK, BLOCK), BF16),
            pltpu.VMEM((4, SAMP, BLOCK, BLOCK), BF16),
            pltpu.VMEM((4, SAMP, BLOCK, BLOCK), BF16),
            pltpu.SemaphoreType.DMA((8, CHUNKS)),
            pltpu.SemaphoreType.DMA((8, CHUNKS)),
            pltpu.SemaphoreType.DMA((2,)),
            pltpu.SemaphoreType.DMA((2,)),
            pltpu.SemaphoreType.DMA((5,)),
            pltpu.SemaphoreType.DMA((5,)),
            pltpu.SemaphoreType.DMA((4,)),
            pltpu.SemaphoreType.DMA((4,)),
            pltpu.SemaphoreType.DMA((6,)),
            pltpu.SemaphoreType.DMA((7,)),
        ],
        compiler_params=pltpu.CompilerParams(
            collective_id=0, has_side_effects=True, vmem_limit_bytes=48 * 1024 * 1024
        ),
    )(
        *(
            pltpu.with_memory_space_constraint(value, pltpu.HBM)
            for value in (
                features.reshape(OWN, BLOCK, width),
                cotangent.reshape(OWN, BLOCK, width),
                right_factor,
                left_factor,
                mixing,
            )
        )
    )
    wide = jax.ShapeDtypeStruct((LAYERS, OWN, BLOCK, BLOCK), F32)
    output, fgrad, gright, gleft, gmix = pl.pallas_call(
        finish,
        out_shape=(acts, acts, wide, wide, jax.ShapeDtypeStruct((LAYERS, 2, OWN, BLOCK), F32)),
        in_specs=[hbm, hbm, vmem, vmem, hbm],
        out_specs=[hbm] * 5,
        scratch_shapes=[
            pltpu.VMEM((2, LAYERS, OWN, BLOCK, BLOCK), F32),
            pltpu.SemaphoreType.DMA((3, LAYERS * OWN)),
        ],
        compiler_params=pltpu.CompilerParams(vmem_limit_bytes=12 * 1024 * 1024),
    )(output, fgrad, gright, gleft, gmix)
    return output.reshape(OWN * BLOCK, width), fgrad.reshape(OWN * BLOCK, width), gright, gleft, gmix


def solution(mesh):
    specs = (
        P(("chan", "bfly"), "samp"),
        P(("chan", "bfly"), "samp"),
        P(None, ("chan", "bfly"), None, None),
        P(None, ("chan", "bfly"), None, None),
        P(None, None, ("chan", "bfly"), None),
    )
    return jax.shard_map(local, mesh=mesh, in_specs=specs, out_specs=specs, check_vma=False)
```

```python
import functools

import jax
import jax.numpy as jnp
from jax import lax
from jax.experimental import pallas as pl
from jax.experimental.pallas import tpu as pltpu
from jax.sharding import PartitionSpec as P

BLOCK = 256
LAYERS = 2
PEERS = 64
OWN = 4
ROWS = 16
GROUPS = 4
GPEERS = PEERS // GROUPS
SAMP = 4
CHUNKS = 2
CUT_A = 50
CUT_B = 20
MESH = pl.DeviceIdType.MESH
F32 = jnp.float32
BF16 = jnp.bfloat16

U1, T1, U2, COT, T2, DU2, E1, DU1 = range(8)
GL2, GR2, GL1, GR1 = range(4)
Q_ROW, Q_ROW_T, Q_COL, Q_COL_T = range(4)


def mm(a, b):
    return lax.dot_general(a, b, (((1,), (0,)), ((), ())), preferred_element_type=F32)


def mm_t(a, b):
    return lax.dot_general(a, b, (((1,), (1,)), ((), ())), preferred_element_type=F32)


def flip(groups):
    parts = []
    for pair in range(GPEERS // 2):
        parts += [groups[2 * pair + 1 : 2 * pair + 2], groups[2 * pair : 2 * pair + 1]]
    return jnp.concatenate(parts, axis=0)


def kernel(
    feat_hbm, cot_hbm, right_hbm, left_hbm, mixing_hbm,
    out_hbm, fgrad_hbm, gright_hbm, gleft_hbm, gmix_ref,
    feat, cot, right, left, mixing, sendb, recvb, qmat, rt, lb, lt, h1, h1d, t1, vn, g1, nat, nat2, dvp, coef, outb, fgradb,
    mixs, mixr, gmacc, gms, gm1, gmy, gacc, gsend, rsr, ag,
    a_send, a_recv, m_send, m_recv, r_send, r_recv, g_send, g_recv, o_sem, i_sem,
):
    samples = h1.shape[3]
    me = lax.axis_index("chan") * 2 + lax.axis_index("bfly")
    y = lax.axis_index("samp")

    def fetch(n, src, dst):
        return pltpu.make_async_copy(src, dst, i_sem.at[n])

    fetches = [
        fetch(2, cot_hbm, cot),
        fetch(0, right_hbm.at[0], right.at[0]),
        fetch(1, feat_hbm, feat),
        fetch(3, left_hbm.at[0], left.at[0]),
        fetch(4, right_hbm.at[1], right.at[1]),
        fetch(5, left_hbm.at[1], left.at[1]),
        fetch(6, mixing_hbm, mixing),
    ]
    for one_fetch in fetches:
        one_fetch.start()
    fetches = [fetches[1], fetches[2], fetches[0]] + fetches[3:]

    def peer_id(p):
        return {"chan": p // 2, "bfly": lax.rem(p, 2)}

    barrier = pltpu.get_barrier_semaphore()

    def greet(k, carry):
        pl.semaphore_signal(barrier, inc=1, device_id=peer_id(lax.rem(me + k, PEERS)), device_id_type=MESH)
        return carry

    lax.fori_loop(1, PEERS, greet, 0)
    for d in range(1, SAMP):
        pl.semaphore_signal(barrier, inc=1, device_id={"samp": lax.rem(y + d, SAMP)}, device_id_type=MESH)

    i0 = lax.broadcasted_iota(jnp.int32, (BLOCK, BLOCK), 0)
    i1 = lax.broadcasted_iota(jnp.int32, (BLOCK, BLOCK), 1)

    def row_of(m):
        return ((m >> 2) & 3) * 64 + (m >> 4) * 4 + (m & 3)

    def col_of(m):
        return (m & 3) * 64 + (m >> 4) * 4 + ((m >> 2) & 3)

    def onehot(mask):
        return jnp.where(mask, 1.0, 0.0).astype(BF16)

    qmat[Q_ROW] = onehot(i1 == row_of(i0))

    def to_peers(which, src, put):
        for g in range(GROUPS):
            x = jnp.concatenate([src[b, 64 * g : 64 * g + 64, :] for b in range(OWN)], axis=0)
            put(g, mm(qmat[which], x))

    def put_into(dst):
        def put(g, value):
            dst[GPEERS * g : GPEERS * (g + 1)] = value.astype(BF16).reshape(GPEERS, ROWS, samples)

        return put

    def split_into(dst, g, value):
        value = value.astype(BF16)
        for b in range(OWN):
            dst[b, 64 * g : 64 * g + 64, :] = value[64 * b : 64 * b + 64]

    def from_peers(which, src, dst):
        for g in range(GROUPS):
            x = src[GPEERS * g : GPEERS * (g + 1)].reshape(BLOCK, samples)
            split_into(dst, g, mm(qmat[which], x))

    def chunk_of(c):
        return pl.ds(pl.multiple_of(c * samples, samples), samples)

    def send(a, c, low=1, high=PEERS):
        def one(k, carry):
            p = lax.rem(me + k, PEERS)
            pltpu.make_async_remote_copy(
                src_ref=sendb.at[a, c, p], dst_ref=recvb.at[a, c, me],
                send_sem=a_send.at[a, c], recv_sem=a_recv.at[a, c],
                device_id=peer_id(p), device_id_type=MESH,
            ).start()
            return carry

        lax.fori_loop(low, high, one, 0)
        if low == 1:
            recvb[a, c, pl.ds(me, 1)] = sendb[a, c, pl.ds(me, 1)]

    def wait_all(ref, sem):
        pltpu.make_async_copy(ref, ref, sem).wait()

    def wait_recv(a, c):
        wait_all(recvb.at[a, c, pl.ds(0, PEERS - 1)], a_recv.at[a, c])

    def first(c):
        for b in range(OWN):
            nat[b] = mm(rt[0, b], feat[b, :, chunk_of(c)]).astype(BF16)
        to_peers(Q_ROW, nat, put_into(sendb.at[U1, c]))

    def first_cot(c):
        for b in range(OWN):
            nat2[b] = cot[b, :, chunk_of(c)]
        to_peers(Q_ROW, nat2, put_into(sendb.at[COT, c]))

    fetches[2].wait()
    first_cot(0)
    pl.semaphore_wait(barrier, PEERS - 1 + SAMP - 1)
    send(COT, 0)
    fetches[0].wait()
    for b in range(OWN):
        rt[0, b] = right[0, b].T
    fetches[1].wait()
    first(0)
    send(U1, 0)

    pick = onehot((lax.broadcasted_iota(jnp.int32, (BLOCK, 128), 0) & 3) == (lax.broadcasted_iota(jnp.int32, (BLOCK, 128), 1) & 3)).astype(F32)
    lane = lax.broadcasted_iota(jnp.int32, (PEERS, 128), 1)
    owner = lax.broadcasted_iota(jnp.int32, (PEERS, BLOCK), 0)
    unit = lax.broadcasted_iota(jnp.int32, (PEERS, BLOCK), 1)
    fetches[6].wait()
    message = jnp.zeros((PEERS, 128), F32)
    for r in range(ROWS):
        row = mixing[r // 8, (r // 4) % 2, r % 4 : r % 4 + 1, :]
        spread = jnp.where((unit >> 2) == owner, jnp.broadcast_to(row, (PEERS, BLOCK)), 0.0)
        found = lax.dot_general(
            spread, pick, (((1,), (0,)), ((), ())), precision=lax.Precision.HIGHEST, preferred_element_type=F32
        )
        message = message + jnp.where((lane >> 2) == r, found, 0.0)
    mixs[...] = message.reshape(PEERS, 1, 128)

    def send_mix(k, carry):
        p = lax.rem(me + k, PEERS)
        pltpu.make_async_remote_copy(
            src_ref=mixs.at[p], dst_ref=mixr.at[me], send_sem=m_send.at[0], recv_sem=m_recv.at[0],
            device_id=peer_id(p), device_id_type=MESH,
        ).start()
        return carry

    lax.fori_loop(1, PEERS, send_mix, 0)
    mixr[pl.ds(me, 1)] = mixs[pl.ds(me, 1)]
    for c in range(1, CHUNKS):
        first(c)
        send(U1, c)

    qmat[Q_ROW_T] = onehot(i0 == row_of(i1))
    qmat[Q_COL] = onehot(i1 == col_of(i0))
    qmat[Q_COL_T] = onehot(i0 == col_of(i1))
    for c in range(1, CHUNKS):
        first_cot(c)
    for n in (3, 4, 5):
        fetches[n].wait()
    for b in range(OWN):
        rt[1, b] = right[1, b].T
        for layer in range(LAYERS):
            lb[layer, b] = left[layer, b].astype(BF16)
            lt[layer, b] = left[layer, b].T.astype(BF16)
    for a in range(4):
        gacc[a] = jnp.zeros((OWN, BLOCK, BLOCK), F32)
    gmacc[...] = jnp.zeros((PEERS, 128), F32)
    wait_all(mixr.at[pl.ds(0, PEERS - 1)], m_recv.at[0])
    lane3 = lax.broadcasted_iota(jnp.int32, (GPEERS, ROWS, 128), 2)
    row3 = lax.broadcasted_iota(jnp.int32, (GPEERS, ROWS, 128), 1)
    for g in range(GROUPS):
        got = jnp.broadcast_to(mixr[GPEERS * g : GPEERS * (g + 1)], (GPEERS, ROWS, 128))
        for term in range(4):
            value = jnp.sum(jnp.where(lane3 == row3 + ROWS * term, got, 0.0), axis=2, keepdims=True)
            coef[term, GPEERS * g : GPEERS * (g + 1)] = jnp.broadcast_to(value, (GPEERS, ROWS, 128))

    def gain(term, g):
        value = coef[term, GPEERS * g : GPEERS * (g + 1)]
        return jnp.concatenate([value] * (samples // 128), axis=2)

    def mix_forward(layer, a, c):
        for g in range(GROUPS):
            u = recvb[a, c, GPEERS * g : GPEERS * (g + 1)].astype(F32)
            v = (gain(2 * layer, g) * u + gain(2 * layer + 1, g) * flip(u)).astype(BF16)
            split_into(vn.at[layer, c], g, mm(qmat[Q_COL_T], v.reshape(BLOCK, samples)))

    def mix_backward(layer, a, c):
        def put(g, value):
            dv = value.reshape(GPEERS, ROWS, samples)
            dvp[GPEERS * g : GPEERS * (g + 1)] = dv.astype(BF16)
            part = (gain(2 * layer + 1, g) * dv).astype(BF16).astype(F32)
            du = gain(2 * layer, g) * dv + flip(part)
            sendb[a, c, GPEERS * g : GPEERS * (g + 1)] = du.astype(BF16)

        to_peers(Q_COL, nat2, put)

    def mix_gradient(layer, a, c):
        for g in range(GROUPS):
            dv = dvp[GPEERS * g : GPEERS * (g + 1)].astype(F32)
            u = recvb[a, c, GPEERS * g : GPEERS * (g + 1)].astype(F32)
            total = jnp.zeros((GPEERS, ROWS, 128), F32)
            for term, other in ((0, u), (1, flip(u))):
                prod = dv * other
                half = prod[:, :, :128]
                for piece in range(1, samples // 128):
                    half = half + prod[:, :, 128 * piece : 128 * (piece + 1)]
                value = jnp.sum(half, axis=2, keepdims=True)
                total = total + jnp.where(
                    lane3 == row3 + ROWS * (2 * layer + term), jnp.broadcast_to(value, (GPEERS, ROWS, 128)), 0.0
                )
            gmacc[GPEERS * g : GPEERS * (g + 1)] += jnp.sum(total, axis=1)

    def scatter(a):
        gsend[a] = gacc[a].astype(BF16)
        for d in range(1, SAMP):
            to = lax.rem(y + d, SAMP)
            pltpu.make_async_remote_copy(
                src_ref=gsend.at[a, to], dst_ref=rsr.at[a, y], send_sem=r_send.at[a], recv_sem=r_recv.at[a],
                device_id={"samp": to}, device_id_type=MESH,
            ).start()

    def gather(a):
        wait_all(rsr.at[a, pl.ds(0, SAMP - 1)], r_recv.at[a])
        total = gacc[a, y]
        for d in range(1, SAMP):
            total = total + rsr[a, lax.rem(y + d, SAMP)].astype(F32)
        ag[a, y] = total.astype(BF16)
        for d in range(1, SAMP):
            to = lax.rem(y + d, SAMP)
            pltpu.make_async_remote_copy(
                src_ref=ag.at[a, y], dst_ref=ag.at[a, y], send_sem=g_send.at[a], recv_sem=g_recv.at[a],
                device_id={"samp": to}, device_id_type=MESH,
            ).start()

    def store(a):
        wait_all(ag.at[a, pl.ds(0, SAMP - 1)], g_recv.at[a])
        dst = (gleft_hbm if a in (GL1, GL2) else gright_hbm).at[0 if a in (GL1, GR1) else 1]
        pltpu.make_async_copy(ag.at[a], dst, o_sem.at[a]).start()

    def col1(c, carry):
        wait_recv(U1, c)
        mix_forward(0, U1, c)
        for j in range(OWN):
            nat[j] = mm(lt[0, j], vn[0, c, j]).astype(BF16)
        to_peers(Q_COL, nat, put_into(sendb.at[T1, c]))
        send(T1, c)
        return carry

    lax.fori_loop(0, CHUNKS, col1, 0)
    for c in range(1, CHUNKS):
        send(COT, c)

    def row2(c, carry):
        wait_recv(T1, c)
        from_peers(Q_ROW_T, recvb.at[T1, c], t1.at[c])
        for b in range(OWN):
            t = t1[c, b].astype(F32)
            h = (feat[b, :, chunk_of(c)].astype(F32) + t * jax.nn.sigmoid(t)).astype(BF16)
            h1[c, b] = h
            nat[b] = mm(rt[1, b], h).astype(BF16)
        to_peers(Q_ROW, nat, put_into(sendb.at[U2, c]))
        send(U2, c)
        return carry

    lax.fori_loop(0, CHUNKS, row2, 0)

    def slope(g, t):
        s = jax.nn.sigmoid(t)
        return (g * s * (1.0 + t * (1.0 - s))).astype(BF16)

    def col2(c):
        wait_recv(COT, c)
        from_peers(Q_COL_T, recvb.at[COT, c], nat2)
        wait_recv(U2, c)
        mix_forward(1, U2, c)
        for j in range(OWN):
            t = mm(lt[1, j], vn[1, c, j]).astype(BF16)
            nat[j] = t
            e = slope(nat2[j].astype(F32), t.astype(F32))
            gacc[GL2, j] += mm_t(vn[1, c, j], e)
            nat2[j] = mm(lb[1, j], e).astype(BF16)
        if c == CHUNKS - 1:
            scatter(GL2)
        mix_backward(1, DU2, c)
        send(DU2, c)
        to_peers(Q_COL, nat, put_into(sendb.at[T2, c]))
        mix_gradient(1, U2, c)

    for c in range(CHUNKS):
        col2(c)

    def row1(c):
        wait_recv(DU2, c)
        from_peers(Q_ROW_T, recvb.at[DU2, c], nat)
        for b in range(OWN):
            g = (cot[b, :, chunk_of(c)].astype(F32) + mm(right[1, b], nat[b])).astype(BF16)
            g1[c, b] = g
            nat2[b] = slope(g.astype(F32), t1[c, b].astype(F32))
        to_peers(Q_ROW, nat2, put_into(sendb.at[E1, c]))

    def row1_grad(c):
        for b in range(OWN):
            gacc[GR2, b] += mm_t(h1[c, b], nat[b])

    row1(0)
    send(E1, 0)
    row1_grad(0)
    gather(GL2)
    row1(1)
    row1_grad(1)
    scatter(GR2)
    send(E1, 1)

    def col1_back(c):
        wait_recv(E1, c)
        from_peers(Q_COL_T, recvb.at[E1, c], nat)
        for j in range(OWN):
            nat2[j] = mm(lb[0, j], nat[j]).astype(BF16)
        mix_backward(0, DU1, c)

    def col1_grad(c):
        for j in range(OWN):
            gacc[GL1, j] += mm_t(vn[0, c, j], nat[j])

    col1_back(0)
    send(DU1, 0)
    col1_grad(0)
    mix_gradient(0, U1, 0)
    gather(GR2)
    col1_back(1)
    col1_grad(1)
    scatter(GL1)
    send(DU1, 1)
    mix_gradient(0, U1, 1)
    store(GL2)
    gms[...] = gmacc[...].reshape(PEERS, 1, 128)

    def send_gm(k, carry):
        p = lax.rem(me + k, PEERS)
        pltpu.make_async_remote_copy(
            src_ref=gms.at[p], dst_ref=gm1.at[me], send_sem=m_send.at[1], recv_sem=m_recv.at[1],
            device_id=peer_id(p), device_id_type=MESH,
        ).start()
        return carry

    lax.fori_loop(1, PEERS, send_gm, 0)
    gm1[pl.ds(me, 1)] = gms[pl.ds(me, 1)]
    store(GR2)
    gather(GL1)
    send(T2, 0, 1, CUT_A)

    dun = h1d

    def row0(c, carry):
        wait_recv(DU1, c)
        from_peers(Q_ROW_T, recvb.at[DU1, c], dun.at[c])
        for b in range(OWN):
            gacc[GR1, b] += mm_t(feat[b, :, chunk_of(c)], dun[c, b])
        return carry

    lax.fori_loop(0, CHUNKS, row0, 0)
    scatter(GR1)
    wait_all(gm1.at[pl.ds(0, PEERS - 1)], m_recv.at[1])
    gmy[pl.ds(y, 1)] = gm1[...].reshape(1, PEERS, 1, 128)
    for d in range(1, SAMP):
        to = lax.rem(y + d, SAMP)
        pltpu.make_async_remote_copy(
            src_ref=gm1, dst_ref=gmy.at[y], send_sem=r_send.at[4], recv_sem=r_recv.at[4],
            device_id={"samp": to}, device_id_type=MESH,
        ).start()
    send(T2, 0, CUT_A, PEERS)
    send(T2, 1, 1, CUT_B)

    def row0_grad(c, carry):
        for b in range(OWN):
            fgradb[b, :, chunk_of(c)] = (g1[c, b].astype(F32) + mm(right[0, b], dun[c, b])).astype(BF16)
        return carry

    lax.fori_loop(0, CHUNKS, row0_grad, 0)
    pltpu.make_async_copy(fgradb, fgrad_hbm, o_sem.at[5]).start()
    store(GL1)
    gather(GR1)
    send(T2, 1, CUT_B, PEERS)
    wait_all(gmy.at[pl.ds(0, SAMP - 1)], r_recv.at[4])
    total = (gmy[0] + gmy[1] + gmy[2] + gmy[3]).reshape(PEERS, 128)
    spread_back = onehot(
        (lax.broadcasted_iota(jnp.int32, (128, BLOCK), 0) & 3) == (lax.broadcasted_iota(jnp.int32, (128, BLOCK), 1) & 3)
    ).astype(F32)
    for r in range(ROWS):
        found = lax.dot_general(
            jnp.where((lane >> 2) == r, total, 0.0), spread_back, (((1,), (0,)), ((), ())),
            precision=lax.Precision.HIGHEST, preferred_element_type=F32,
        )
        gmix_ref[r // 8, (r // 4) % 2, r % 4 : r % 4 + 1, :] = jnp.sum(
            jnp.where((unit >> 2) == owner, found, 0.0), axis=0, keepdims=True
        )

    def final_output(c, carry):
        wait_recv(T2, c)
        from_peers(Q_ROW_T, recvb.at[T2, c], nat)
        for b in range(OWN):
            t = nat[b].astype(F32)
            outb[b, :, chunk_of(c)] = (h1[c, b].astype(F32) + t * jax.nn.sigmoid(t)).astype(BF16)
        return carry

    lax.fori_loop(0, CHUNKS, final_output, 0)
    pltpu.make_async_copy(outb, out_hbm, o_sem.at[4]).start()
    store(GR1)

    for a in range(8):
        for c in range(CHUNKS):
            wait_all(sendb.at[a, c, pl.ds(0, PEERS - 1)], a_send.at[a, c])
    wait_all(mixs.at[pl.ds(0, PEERS - 1)], m_send.at[0])
    wait_all(gms.at[pl.ds(0, PEERS - 1)], m_send.at[1])
    for a in range(4):
        wait_all(gsend.at[a, pl.ds(0, SAMP - 1)], r_send.at[a])
        wait_all(ag.at[a, pl.ds(0, SAMP - 1)], g_send.at[a])
        wait_all(ag.at[a], o_sem.at[a])
    wait_all(gmy.at[pl.ds(0, SAMP - 1)], r_send.at[4])
    wait_all(outb, o_sem.at[4])
    wait_all(fgradb, o_sem.at[5])


def finish(out_in, fgrad_in, gright_in, gleft_in, gmix_in, out, fgrad, gright, gleft, gmix, wide, sem):
    whole = [
        pltpu.make_async_copy(src, dst, sem.at[0, n])
        for n, (src, dst) in enumerate(((out_in, out), (fgrad_in, fgrad), (gmix_in, gmix)))
    ]
    for copy in whole:
        copy.start()
    pieces = []
    for n, (src, dst) in enumerate(((gright_in, gright), (gleft_in, gleft))):
        for layer in range(LAYERS):
            for b in range(OWN):
                wide[n, layer, b] = src[layer, b].astype(F32)
                copy = pltpu.make_async_copy(wide.at[n, layer, b], dst.at[layer, b], sem.at[1 + n, OWN * layer + b])
                copy.start()
                pieces.append(copy)
    for copy in whole + pieces:
        copy.wait()


def local(features, cotangent, right_factor, left_factor, mixing):
    width = features.shape[1]
    samples = width // CHUNKS
    vmem = pl.BlockSpec(memory_space=pltpu.VMEM)
    hbm = pl.BlockSpec(memory_space=pl.ANY)
    acts = jax.ShapeDtypeStruct((OWN, BLOCK, width), BF16)
    grads = jax.ShapeDtypeStruct((LAYERS, OWN, BLOCK, BLOCK), BF16)
    chunked = pltpu.VMEM((CHUNKS, OWN, BLOCK, samples), BF16)
    small = pltpu.VMEM((PEERS, 1, 128), F32)
    output, fgrad, gright, gleft, gmix = pl.pallas_call(
        kernel,
        out_shape=(acts, acts, grads, grads, jax.ShapeDtypeStruct((LAYERS, 2, OWN, BLOCK), F32)),
        in_specs=[pl.BlockSpec(memory_space=pltpu.HBM)] * 5,
        out_specs=(hbm, hbm, hbm, hbm, vmem),
        scratch_shapes=[
            pltpu.VMEM((OWN, BLOCK, width), BF16),
            pltpu.VMEM((OWN, BLOCK, width), BF16),
            pltpu.VMEM((LAYERS, OWN, BLOCK, BLOCK), BF16),
            pltpu.VMEM((LAYERS, OWN, BLOCK, BLOCK), F32),
            pltpu.VMEM((LAYERS, 2, OWN, BLOCK), F32),
            pltpu.VMEM((8, CHUNKS, PEERS, ROWS, samples), BF16),
            pltpu.VMEM((8, CHUNKS, PEERS, ROWS, samples), BF16),
            pltpu.VMEM((4, BLOCK, BLOCK), BF16),
            pltpu.VMEM((LAYERS, OWN, BLOCK, BLOCK), BF16),
            pltpu.VMEM((LAYERS, OWN, BLOCK, BLOCK), BF16),
            pltpu.VMEM((LAYERS, OWN, BLOCK, BLOCK), BF16),
            chunked,
            chunked,
            chunked,
            pltpu.VMEM((LAYERS, CHUNKS, OWN, BLOCK, samples), BF16),
            chunked,
            pltpu.VMEM((OWN, BLOCK, samples), BF16),
            pltpu.VMEM((OWN, BLOCK, samples), BF16),
            pltpu.VMEM((PEERS, ROWS, samples), BF16),
            pltpu.VMEM((4, PEERS, ROWS, 128), F32),
            pltpu.VMEM((OWN, BLOCK, width), BF16),
            pltpu.VMEM((OWN, BLOCK, width), BF16),
            small,
            small,
            pltpu.VMEM((PEERS, 128), F32),
            small,
            small,
            pltpu.VMEM((SAMP, PEERS, 1, 128), F32),
            pltpu.VMEM((4, OWN, BLOCK, BLOCK), F32),
            pltpu.VMEM((4, OWN, BLOCK, BLOCK), BF16),
            pltpu.VMEM((4, SAMP, BLOCK, BLOCK), BF16),
            pltpu.VMEM((4, SAMP, BLOCK, BLOCK), BF16),
            pltpu.SemaphoreType.DMA((8, CHUNKS)),
            pltpu.SemaphoreType.DMA((8, CHUNKS)),
            pltpu.SemaphoreType.DMA((2,)),
            pltpu.SemaphoreType.DMA((2,)),
            pltpu.SemaphoreType.DMA((5,)),
            pltpu.SemaphoreType.DMA((5,)),
            pltpu.SemaphoreType.DMA((4,)),
            pltpu.SemaphoreType.DMA((4,)),
            pltpu.SemaphoreType.DMA((6,)),
            pltpu.SemaphoreType.DMA((7,)),
        ],
        compiler_params=pltpu.CompilerParams(
            collective_id=0, has_side_effects=True, vmem_limit_bytes=48 * 1024 * 1024
        ),
    )(
        *(
            pltpu.with_memory_space_constraint(value, pltpu.HBM)
            for value in (
                features.reshape(OWN, BLOCK, width),
                cotangent.reshape(OWN, BLOCK, width),
                right_factor,
                left_factor,
                mixing,
            )
        )
    )
    wide = jax.ShapeDtypeStruct((LAYERS, OWN, BLOCK, BLOCK), F32)
    output, fgrad, gright, gleft, gmix = pl.pallas_call(
        finish,
        out_shape=(acts, acts, wide, wide, jax.ShapeDtypeStruct((LAYERS, 2, OWN, BLOCK), F32)),
        in_specs=[hbm, hbm, vmem, vmem, hbm],
        out_specs=[hbm] * 5,
        scratch_shapes=[
            pltpu.VMEM((2, LAYERS, OWN, BLOCK, BLOCK), F32),
            pltpu.SemaphoreType.DMA((3, LAYERS * OWN)),
        ],
        compiler_params=pltpu.CompilerParams(vmem_limit_bytes=12 * 1024 * 1024),
    )(output, fgrad, gright, gleft, gmix)
    return output.reshape(OWN * BLOCK, width), fgrad.reshape(OWN * BLOCK, width), gright, gleft, gmix


def solution(mesh):
    specs = (
        P(("chan", "bfly"), "samp"),
        P(("chan", "bfly"), "samp"),
        P(None, ("chan", "bfly"), None, None),
        P(None, ("chan", "bfly"), None, None),
        P(None, None, ("chan", "bfly"), None),
    )
    return jax.shard_map(local, mesh=mesh, in_specs=specs, out_specs=specs, check_vma=False)
```

```python
import functools

import jax
import jax.numpy as jnp
from jax import lax
from jax.experimental import pallas as pl
from jax.experimental.pallas import tpu as pltpu
from jax.sharding import PartitionSpec as P

BLOCK = 256
LAYERS = 2
PEERS = 64
OWN = 4
ROWS = 16
GROUPS = 4
GPEERS = PEERS // GROUPS
SAMP = 4
CHUNKS = 2
TAIL_CUT = 33
MESH = pl.DeviceIdType.MESH
F32 = jnp.float32
BF16 = jnp.bfloat16

U1, T1, U2, COT, T2, DU2, E1, DU1 = range(8)
GL2, GR2, GL1, GR1 = range(4)
Q_ROW, Q_ROW_T, Q_COL, Q_COL_T = range(4)


def mm(a, b):
    return lax.dot_general(a, b, (((1,), (0,)), ((), ())), preferred_element_type=F32)


def mm_t(a, b):
    return lax.dot_general(a, b, (((1,), (1,)), ((), ())), preferred_element_type=F32)


def flip(groups):
    parts = []
    for pair in range(GPEERS // 2):
        parts += [groups[2 * pair + 1 : 2 * pair + 2], groups[2 * pair : 2 * pair + 1]]
    return jnp.concatenate(parts, axis=0)


def kernel(
    feat_hbm, cot_hbm, right_hbm, left_hbm, mixing_hbm,
    out_hbm, fgrad_hbm, gright_hbm, gleft_hbm, gmix_ref,
    feat, cot, right, left, mixing, sendb, recvb, qmat, rt, lb, lt, h1, h1d, t1, vn, g1, nat, nat2, dvp, coef, outb, fgradb,
    mixs, mixr, gmacc, gms, gm1, gmy, gacc, gsend, rsr, ag,
    a_send, a_recv, m_send, m_recv, r_send, r_recv, g_send, g_recv, o_sem, i_sem,
):
    samples = h1.shape[3]
    me = lax.axis_index("chan") * 2 + lax.axis_index("bfly")
    y = lax.axis_index("samp")

    def fetch(n, src, dst):
        return pltpu.make_async_copy(src, dst, i_sem.at[n])

    fetches = [
        fetch(2, cot_hbm, cot),
        fetch(0, right_hbm.at[0], right.at[0]),
        fetch(1, feat_hbm, feat),
        fetch(3, left_hbm.at[0], left.at[0]),
        fetch(4, right_hbm.at[1], right.at[1]),
        fetch(5, left_hbm.at[1], left.at[1]),
        fetch(6, mixing_hbm, mixing),
    ]
    for one_fetch in fetches:
        one_fetch.start()
    fetches = [fetches[1], fetches[2], fetches[0]] + fetches[3:]

    def peer_id(p):
        return {"chan": p // 2, "bfly": lax.rem(p, 2)}

    barrier = pltpu.get_barrier_semaphore()

    def greet(k, carry):
        pl.semaphore_signal(barrier, inc=1, device_id=peer_id(lax.rem(me + k, PEERS)), device_id_type=MESH)
        return carry

    lax.fori_loop(1, PEERS, greet, 0)
    for d in range(1, SAMP):
        pl.semaphore_signal(barrier, inc=1, device_id={"samp": lax.rem(y + d, SAMP)}, device_id_type=MESH)

    i0 = lax.broadcasted_iota(jnp.int32, (BLOCK, BLOCK), 0)
    i1 = lax.broadcasted_iota(jnp.int32, (BLOCK, BLOCK), 1)

    def row_of(m):
        return ((m >> 2) & 3) * 64 + (m >> 4) * 4 + (m & 3)

    def col_of(m):
        return (m & 3) * 64 + (m >> 4) * 4 + ((m >> 2) & 3)

    def onehot(mask):
        return jnp.where(mask, 1.0, 0.0).astype(BF16)

    qmat[Q_ROW] = onehot(i1 == row_of(i0))

    def to_peers(which, src, put):
        for g in range(GROUPS):
            x = jnp.concatenate([src[b, 64 * g : 64 * g + 64, :] for b in range(OWN)], axis=0)
            put(g, mm(qmat[which], x))

    def put_into(dst):
        def put(g, value):
            dst[GPEERS * g : GPEERS * (g + 1)] = value.astype(BF16).reshape(GPEERS, ROWS, samples)

        return put

    def split_into(dst, g, value):
        value = value.astype(BF16)
        for b in range(OWN):
            dst[b, 64 * g : 64 * g + 64, :] = value[64 * b : 64 * b + 64]

    def from_peers(which, src, dst):
        for g in range(GROUPS):
            x = src[GPEERS * g : GPEERS * (g + 1)].reshape(BLOCK, samples)
            split_into(dst, g, mm(qmat[which], x))

    def chunk_of(c):
        return pl.ds(pl.multiple_of(c * samples, samples), samples)

    def send(a, c, low=1, high=PEERS):
        def one(k, carry):
            p = lax.rem(me + k, PEERS)
            pltpu.make_async_remote_copy(
                src_ref=sendb.at[a, c, p], dst_ref=recvb.at[a, c, me],
                send_sem=a_send.at[a, c], recv_sem=a_recv.at[a, c],
                device_id=peer_id(p), device_id_type=MESH,
            ).start()
            return carry

        lax.fori_loop(low, high, one, 0)
        if low == 1:
            recvb[a, c, pl.ds(me, 1)] = sendb[a, c, pl.ds(me, 1)]

    def wait_all(ref, sem):
        pltpu.make_async_copy(ref, ref, sem).wait()

    def wait_recv(a, c):
        wait_all(recvb.at[a, c, pl.ds(0, PEERS - 1)], a_recv.at[a, c])

    def first(c):
        for b in range(OWN):
            nat[b] = mm(rt[0, b], feat[b, :, chunk_of(c)]).astype(BF16)
        to_peers(Q_ROW, nat, put_into(sendb.at[U1, c]))

    def first_cot(c):
        for b in range(OWN):
            nat2[b] = cot[b, :, chunk_of(c)]
        to_peers(Q_ROW, nat2, put_into(sendb.at[COT, c]))

    fetches[2].wait()
    first_cot(0)
    pl.semaphore_wait(barrier, PEERS - 1 + SAMP - 1)
    send(COT, 0)
    fetches[0].wait()
    for b in range(OWN):
        rt[0, b] = right[0, b].T
    fetches[1].wait()
    first(0)
    send(U1, 0)

    pick = onehot((lax.broadcasted_iota(jnp.int32, (BLOCK, 128), 0) & 3) == (lax.broadcasted_iota(jnp.int32, (BLOCK, 128), 1) & 3)).astype(F32)
    lane = lax.broadcasted_iota(jnp.int32, (PEERS, 128), 1)
    owner = lax.broadcasted_iota(jnp.int32, (PEERS, BLOCK), 0)
    unit = lax.broadcasted_iota(jnp.int32, (PEERS, BLOCK), 1)
    fetches[6].wait()
    message = jnp.zeros((PEERS, 128), F32)
    for r in range(ROWS):
        row = mixing[r // 8, (r // 4) % 2, r % 4 : r % 4 + 1, :]
        spread = jnp.where((unit >> 2) == owner, jnp.broadcast_to(row, (PEERS, BLOCK)), 0.0)
        found = lax.dot_general(
            spread, pick, (((1,), (0,)), ((), ())), precision=lax.Precision.HIGHEST, preferred_element_type=F32
        )
        message = message + jnp.where((lane >> 2) == r, found, 0.0)
    mixs[...] = message.reshape(PEERS, 1, 128)

    def send_mix(k, carry):
        p = lax.rem(me + k, PEERS)
        pltpu.make_async_remote_copy(
            src_ref=mixs.at[p], dst_ref=mixr.at[me], send_sem=m_send.at[0], recv_sem=m_recv.at[0],
            device_id=peer_id(p), device_id_type=MESH,
        ).start()
        return carry

    lax.fori_loop(1, PEERS, send_mix, 0)
    mixr[pl.ds(me, 1)] = mixs[pl.ds(me, 1)]
    for c in range(1, CHUNKS):
        first(c)
        send(U1, c)

    qmat[Q_ROW_T] = onehot(i0 == row_of(i1))
    qmat[Q_COL] = onehot(i1 == col_of(i0))
    qmat[Q_COL_T] = onehot(i0 == col_of(i1))
    for c in range(1, CHUNKS):
        first_cot(c)
    for n in (3, 4, 5):
        fetches[n].wait()
    for b in range(OWN):
        rt[1, b] = right[1, b].T
        for layer in range(LAYERS):
            lb[layer, b] = left[layer, b].astype(BF16)
            lt[layer, b] = left[layer, b].T.astype(BF16)
    for a in range(4):
        gacc[a] = jnp.zeros((OWN, BLOCK, BLOCK), F32)
    gmacc[...] = jnp.zeros((PEERS, 128), F32)
    wait_all(mixr.at[pl.ds(0, PEERS - 1)], m_recv.at[0])
    lane3 = lax.broadcasted_iota(jnp.int32, (GPEERS, ROWS, 128), 2)
    row3 = lax.broadcasted_iota(jnp.int32, (GPEERS, ROWS, 128), 1)
    for g in range(GROUPS):
        got = jnp.broadcast_to(mixr[GPEERS * g : GPEERS * (g + 1)], (GPEERS, ROWS, 128))
        for term in range(4):
            value = jnp.sum(jnp.where(lane3 == row3 + ROWS * term, got, 0.0), axis=2, keepdims=True)
            coef[term, GPEERS * g : GPEERS * (g + 1)] = jnp.broadcast_to(value, (GPEERS, ROWS, 128))

    def gain(term, g):
        value = coef[term, GPEERS * g : GPEERS * (g + 1)]
        return jnp.concatenate([value] * (samples // 128), axis=2)

    def mix_forward(layer, a, c):
        for g in range(GROUPS):
            u = recvb[a, c, GPEERS * g : GPEERS * (g + 1)].astype(F32)
            v = (gain(2 * layer, g) * u + gain(2 * layer + 1, g) * flip(u)).astype(BF16)
            split_into(vn.at[layer, c], g, mm(qmat[Q_COL_T], v.reshape(BLOCK, samples)))

    def mix_backward(layer, a, c):
        def put(g, value):
            dv = value.reshape(GPEERS, ROWS, samples)
            dvp[GPEERS * g : GPEERS * (g + 1)] = dv.astype(BF16)
            part = (gain(2 * layer + 1, g) * dv).astype(BF16).astype(F32)
            du = gain(2 * layer, g) * dv + flip(part)
            sendb[a, c, GPEERS * g : GPEERS * (g + 1)] = du.astype(BF16)

        to_peers(Q_COL, nat2, put)

    def mix_gradient(layer, a, c):
        for g in range(GROUPS):
            dv = dvp[GPEERS * g : GPEERS * (g + 1)].astype(F32)
            u = recvb[a, c, GPEERS * g : GPEERS * (g + 1)].astype(F32)
            total = jnp.zeros((GPEERS, ROWS, 128), F32)
            for term, other in ((0, u), (1, flip(u))):
                prod = dv * other
                half = prod[:, :, :128]
                for piece in range(1, samples // 128):
                    half = half + prod[:, :, 128 * piece : 128 * (piece + 1)]
                value = jnp.sum(half, axis=2, keepdims=True)
                total = total + jnp.where(
                    lane3 == row3 + ROWS * (2 * layer + term), jnp.broadcast_to(value, (GPEERS, ROWS, 128)), 0.0
                )
            gmacc[GPEERS * g : GPEERS * (g + 1)] += jnp.sum(total, axis=1)

    def scatter(a):
        gsend[a] = gacc[a].astype(BF16)
        for d in range(1, SAMP):
            to = lax.rem(y + d, SAMP)
            pltpu.make_async_remote_copy(
                src_ref=gsend.at[a, to], dst_ref=rsr.at[a, y], send_sem=r_send.at[a], recv_sem=r_recv.at[a],
                device_id={"samp": to}, device_id_type=MESH,
            ).start()

    def gather(a):
        wait_all(rsr.at[a, pl.ds(0, SAMP - 1)], r_recv.at[a])
        total = gacc[a, y]
        for d in range(1, SAMP):
            total = total + rsr[a, lax.rem(y + d, SAMP)].astype(F32)
        ag[a, y] = total.astype(BF16)
        for d in range(1, SAMP):
            to = lax.rem(y + d, SAMP)
            pltpu.make_async_remote_copy(
                src_ref=ag.at[a, y], dst_ref=ag.at[a, y], send_sem=g_send.at[a], recv_sem=g_recv.at[a],
                device_id={"samp": to}, device_id_type=MESH,
            ).start()

    def store(a):
        wait_all(ag.at[a, pl.ds(0, SAMP - 1)], g_recv.at[a])
        dst = (gleft_hbm if a in (GL1, GL2) else gright_hbm).at[0 if a in (GL1, GR1) else 1]
        pltpu.make_async_copy(ag.at[a], dst, o_sem.at[a]).start()

    def col1(c, carry):
        wait_recv(U1, c)
        mix_forward(0, U1, c)
        for j in range(OWN):
            nat[j] = mm(lt[0, j], vn[0, c, j]).astype(BF16)
        to_peers(Q_COL, nat, put_into(sendb.at[T1, c]))
        send(T1, c)
        return carry

    lax.fori_loop(0, CHUNKS, col1, 0)
    for c in range(1, CHUNKS):
        send(COT, c)

    def row2(c, carry):
        wait_recv(T1, c)
        from_peers(Q_ROW_T, recvb.at[T1, c], t1.at[c])
        for b in range(OWN):
            t = t1[c, b].astype(F32)
            h = (feat[b, :, chunk_of(c)].astype(F32) + t * jax.nn.sigmoid(t)).astype(BF16)
            h1[c, b] = h
            nat[b] = mm(rt[1, b], h).astype(BF16)
        to_peers(Q_ROW, nat, put_into(sendb.at[U2, c]))
        send(U2, c)
        return carry

    lax.fori_loop(0, CHUNKS, row2, 0)

    def slope(g, t):
        s = jax.nn.sigmoid(t)
        return (g * s * (1.0 + t * (1.0 - s))).astype(BF16)

    def col2(c):
        wait_recv(COT, c)
        from_peers(Q_COL_T, recvb.at[COT, c], nat2)
        wait_recv(U2, c)
        mix_forward(1, U2, c)
        for j in range(OWN):
            t = mm(lt[1, j], vn[1, c, j]).astype(BF16)
            nat[j] = t
            e = slope(nat2[j].astype(F32), t.astype(F32))
            gacc[GL2, j] += mm_t(vn[1, c, j], e)
            nat2[j] = mm(lb[1, j], e).astype(BF16)
        if c == CHUNKS - 1:
            scatter(GL2)
        mix_backward(1, DU2, c)
        send(DU2, c)
        to_peers(Q_COL, nat, put_into(sendb.at[T2, c]))
        mix_gradient(1, U2, c)

    for c in range(CHUNKS):
        col2(c)

    def row1(c):
        wait_recv(DU2, c)
        from_peers(Q_ROW_T, recvb.at[DU2, c], nat)
        for b in range(OWN):
            g = (cot[b, :, chunk_of(c)].astype(F32) + mm(right[1, b], nat[b])).astype(BF16)
            g1[c, b] = g
            nat2[b] = slope(g.astype(F32), t1[c, b].astype(F32))
        to_peers(Q_ROW, nat2, put_into(sendb.at[E1, c]))

    def row1_grad(c):
        for b in range(OWN):
            gacc[GR2, b] += mm_t(h1[c, b], nat[b])

    row1(0)
    send(E1, 0)
    row1_grad(0)
    gather(GL2)
    row1(1)
    row1_grad(1)
    scatter(GR2)
    send(E1, 1)

    def col1_back(c):
        wait_recv(E1, c)
        from_peers(Q_COL_T, recvb.at[E1, c], nat)
        for j in range(OWN):
            nat2[j] = mm(lb[0, j], nat[j]).astype(BF16)
        mix_backward(0, DU1, c)

    def col1_grad(c):
        for j in range(OWN):
            gacc[GL1, j] += mm_t(vn[0, c, j], nat[j])

    col1_back(0)
    send(DU1, 0)
    col1_grad(0)
    mix_gradient(0, U1, 0)
    gather(GR2)
    col1_back(1)
    col1_grad(1)
    scatter(GL1)
    send(DU1, 1)
    mix_gradient(0, U1, 1)
    store(GL2)
    gms[...] = gmacc[...].reshape(PEERS, 1, 128)

    def send_gm(k, carry):
        p = lax.rem(me + k, PEERS)
        pltpu.make_async_remote_copy(
            src_ref=gms.at[p], dst_ref=gm1.at[me], send_sem=m_send.at[1], recv_sem=m_recv.at[1],
            device_id=peer_id(p), device_id_type=MESH,
        ).start()
        return carry

    lax.fori_loop(1, PEERS, send_gm, 0)
    gm1[pl.ds(me, 1)] = gms[pl.ds(me, 1)]
    store(GR2)
    gather(GL1)
    send(T2, 0)

    dun = h1d

    def row0(c, carry):
        wait_recv(DU1, c)
        from_peers(Q_ROW_T, recvb.at[DU1, c], dun.at[c])
        for b in range(OWN):
            gacc[GR1, b] += mm_t(feat[b, :, chunk_of(c)], dun[c, b])
        return carry

    lax.fori_loop(0, CHUNKS, row0, 0)
    scatter(GR1)
    wait_all(gm1.at[pl.ds(0, PEERS - 1)], m_recv.at[1])
    gmy[pl.ds(y, 1)] = gm1[...].reshape(1, PEERS, 1, 128)
    for d in range(1, SAMP):
        to = lax.rem(y + d, SAMP)
        pltpu.make_async_remote_copy(
            src_ref=gm1, dst_ref=gmy.at[y], send_sem=r_send.at[4], recv_sem=r_recv.at[4],
            device_id={"samp": to}, device_id_type=MESH,
        ).start()
    send(T2, 1, 1, TAIL_CUT)

    def row0_grad(c, carry):
        for b in range(OWN):
            fgradb[b, :, chunk_of(c)] = (g1[c, b].astype(F32) + mm(right[0, b], dun[c, b])).astype(BF16)
        return carry

    lax.fori_loop(0, CHUNKS, row0_grad, 0)
    pltpu.make_async_copy(fgradb, fgrad_hbm, o_sem.at[5]).start()
    store(GL1)
    gather(GR1)
    send(T2, 1, TAIL_CUT, PEERS)
    wait_all(gmy.at[pl.ds(0, SAMP - 1)], r_recv.at[4])
    total = (gmy[0] + gmy[1] + gmy[2] + gmy[3]).reshape(PEERS, 128)
    spread_back = onehot(
        (lax.broadcasted_iota(jnp.int32, (128, BLOCK), 0) & 3) == (lax.broadcasted_iota(jnp.int32, (128, BLOCK), 1) & 3)
    ).astype(F32)
    for r in range(ROWS):
        found = lax.dot_general(
            jnp.where((lane >> 2) == r, total, 0.0), spread_back, (((1,), (0,)), ((), ())),
            precision=lax.Precision.HIGHEST, preferred_element_type=F32,
        )
        gmix_ref[r // 8, (r // 4) % 2, r % 4 : r % 4 + 1, :] = jnp.sum(
            jnp.where((unit >> 2) == owner, found, 0.0), axis=0, keepdims=True
        )

    def final_output(c, carry):
        wait_recv(T2, c)
        from_peers(Q_ROW_T, recvb.at[T2, c], nat)
        for b in range(OWN):
            t = nat[b].astype(F32)
            outb[b, :, chunk_of(c)] = (h1[c, b].astype(F32) + t * jax.nn.sigmoid(t)).astype(BF16)
        return carry

    final_output(0, 0)
    store(GR1)
    final_output(1, 0)
    pltpu.make_async_copy(outb, out_hbm, o_sem.at[4]).start()

    for a in range(8):
        for c in range(CHUNKS):
            wait_all(sendb.at[a, c, pl.ds(0, PEERS - 1)], a_send.at[a, c])
    wait_all(mixs.at[pl.ds(0, PEERS - 1)], m_send.at[0])
    wait_all(gms.at[pl.ds(0, PEERS - 1)], m_send.at[1])
    for a in range(4):
        wait_all(gsend.at[a, pl.ds(0, SAMP - 1)], r_send.at[a])
        wait_all(ag.at[a, pl.ds(0, SAMP - 1)], g_send.at[a])
        wait_all(ag.at[a], o_sem.at[a])
    wait_all(gmy.at[pl.ds(0, SAMP - 1)], r_send.at[4])
    wait_all(outb, o_sem.at[4])
    wait_all(fgradb, o_sem.at[5])


def finish(out_in, fgrad_in, gright_in, gleft_in, gmix_in, out, fgrad, gright, gleft, gmix, wide, sem):
    whole = [
        pltpu.make_async_copy(src, dst, sem.at[0, n])
        for n, (src, dst) in enumerate(((out_in, out), (fgrad_in, fgrad), (gmix_in, gmix)))
    ]
    for copy in whole:
        copy.start()
    pieces = []
    for n, (src, dst) in enumerate(((gright_in, gright), (gleft_in, gleft))):
        for layer in range(LAYERS):
            for b in range(OWN):
                wide[n, layer, b] = src[layer, b].astype(F32)
                copy = pltpu.make_async_copy(wide.at[n, layer, b], dst.at[layer, b], sem.at[1 + n, OWN * layer + b])
                copy.start()
                pieces.append(copy)
    for copy in whole + pieces:
        copy.wait()


def local(features, cotangent, right_factor, left_factor, mixing):
    width = features.shape[1]
    samples = width // CHUNKS
    vmem = pl.BlockSpec(memory_space=pltpu.VMEM)
    hbm = pl.BlockSpec(memory_space=pl.ANY)
    acts = jax.ShapeDtypeStruct((OWN, BLOCK, width), BF16)
    grads = jax.ShapeDtypeStruct((LAYERS, OWN, BLOCK, BLOCK), BF16)
    chunked = pltpu.VMEM((CHUNKS, OWN, BLOCK, samples), BF16)
    small = pltpu.VMEM((PEERS, 1, 128), F32)
    output, fgrad, gright, gleft, gmix = pl.pallas_call(
        kernel,
        out_shape=(acts, acts, grads, grads, jax.ShapeDtypeStruct((LAYERS, 2, OWN, BLOCK), F32)),
        in_specs=[pl.BlockSpec(memory_space=pltpu.HBM)] * 5,
        out_specs=(hbm, hbm, hbm, hbm, vmem),
        scratch_shapes=[
            pltpu.VMEM((OWN, BLOCK, width), BF16),
            pltpu.VMEM((OWN, BLOCK, width), BF16),
            pltpu.VMEM((LAYERS, OWN, BLOCK, BLOCK), BF16),
            pltpu.VMEM((LAYERS, OWN, BLOCK, BLOCK), F32),
            pltpu.VMEM((LAYERS, 2, OWN, BLOCK), F32),
            pltpu.VMEM((8, CHUNKS, PEERS, ROWS, samples), BF16),
            pltpu.VMEM((8, CHUNKS, PEERS, ROWS, samples), BF16),
            pltpu.VMEM((4, BLOCK, BLOCK), BF16),
            pltpu.VMEM((LAYERS, OWN, BLOCK, BLOCK), BF16),
            pltpu.VMEM((LAYERS, OWN, BLOCK, BLOCK), BF16),
            pltpu.VMEM((LAYERS, OWN, BLOCK, BLOCK), BF16),
            chunked,
            chunked,
            chunked,
            pltpu.VMEM((LAYERS, CHUNKS, OWN, BLOCK, samples), BF16),
            chunked,
            pltpu.VMEM((OWN, BLOCK, samples), BF16),
            pltpu.VMEM((OWN, BLOCK, samples), BF16),
            pltpu.VMEM((PEERS, ROWS, samples), BF16),
            pltpu.VMEM((4, PEERS, ROWS, 128), F32),
            pltpu.VMEM((OWN, BLOCK, width), BF16),
            pltpu.VMEM((OWN, BLOCK, width), BF16),
            small,
            small,
            pltpu.VMEM((PEERS, 128), F32),
            small,
            small,
            pltpu.VMEM((SAMP, PEERS, 1, 128), F32),
            pltpu.VMEM((4, OWN, BLOCK, BLOCK), F32),
            pltpu.VMEM((4, OWN, BLOCK, BLOCK), BF16),
            pltpu.VMEM((4, SAMP, BLOCK, BLOCK), BF16),
            pltpu.VMEM((4, SAMP, BLOCK, BLOCK), BF16),
            pltpu.SemaphoreType.DMA((8, CHUNKS)),
            pltpu.SemaphoreType.DMA((8, CHUNKS)),
            pltpu.SemaphoreType.DMA((2,)),
            pltpu.SemaphoreType.DMA((2,)),
            pltpu.SemaphoreType.DMA((5,)),
            pltpu.SemaphoreType.DMA((5,)),
            pltpu.SemaphoreType.DMA((4,)),
            pltpu.SemaphoreType.DMA((4,)),
            pltpu.SemaphoreType.DMA((6,)),
            pltpu.SemaphoreType.DMA((7,)),
        ],
        compiler_params=pltpu.CompilerParams(
            collective_id=0, has_side_effects=True, vmem_limit_bytes=48 * 1024 * 1024
        ),
    )(
        *(
            pltpu.with_memory_space_constraint(value, pltpu.HBM)
            for value in (
                features.reshape(OWN, BLOCK, width),
                cotangent.reshape(OWN, BLOCK, width),
                right_factor,
                left_factor,
                mixing,
            )
        )
    )
    wide = jax.ShapeDtypeStruct((LAYERS, OWN, BLOCK, BLOCK), F32)
    output, fgrad, gright, gleft, gmix = pl.pallas_call(
        finish,
        out_shape=(acts, acts, wide, wide, jax.ShapeDtypeStruct((LAYERS, 2, OWN, BLOCK), F32)),
        in_specs=[hbm, hbm, vmem, vmem, hbm],
        out_specs=[hbm] * 5,
        scratch_shapes=[
            pltpu.VMEM((2, LAYERS, OWN, BLOCK, BLOCK), F32),
            pltpu.SemaphoreType.DMA((3, LAYERS * OWN)),
        ],
        compiler_params=pltpu.CompilerParams(vmem_limit_bytes=12 * 1024 * 1024),
    )(output, fgrad, gright, gleft, gmix)
    return output.reshape(OWN * BLOCK, width), fgrad.reshape(OWN * BLOCK, width), gright, gleft, gmix


def solution(mesh):
    specs = (
        P(("chan", "bfly"), "samp"),
        P(("chan", "bfly"), "samp"),
        P(None, ("chan", "bfly"), None, None),
        P(None, ("chan", "bfly"), None, None),
        P(None, None, ("chan", "bfly"), None),
    )
    return jax.shard_map(local, mesh=mesh, in_specs=specs, out_specs=specs, check_vma=False)
```

```python
import functools

import jax
import jax.numpy as jnp
from jax import lax
from jax.experimental import pallas as pl
from jax.experimental.pallas import tpu as pltpu
from jax.sharding import PartitionSpec as P

BLOCK = 256
LAYERS = 2
PEERS = 64
OWN = 4
ROWS = 16
GROUPS = 4
GPEERS = PEERS // GROUPS
SAMP = 4
CHUNKS = 2
TAIL_CUT = 33
MESH = pl.DeviceIdType.MESH
F32 = jnp.float32
BF16 = jnp.bfloat16

U1, T1, U2, COT, T2, DU2, E1, DU1 = range(8)
GL2, GR2, GL1, GR1 = range(4)
Q_ROW, Q_ROW_T, Q_COL, Q_COL_T = range(4)


def mm(a, b):
    return lax.dot_general(a, b, (((1,), (0,)), ((), ())), preferred_element_type=F32)


def mm_t(a, b):
    return lax.dot_general(a, b, (((1,), (1,)), ((), ())), preferred_element_type=F32)


def flip(groups):
    parts = []
    for pair in range(GPEERS // 2):
        parts += [groups[2 * pair + 1 : 2 * pair + 2], groups[2 * pair : 2 * pair + 1]]
    return jnp.concatenate(parts, axis=0)


def kernel(
    feat_hbm, cot_hbm, right_hbm, left_hbm, mixing_hbm,
    out_hbm, fgrad_hbm, gright_hbm, gleft_hbm, gmix_ref,
    feat, cot, right, left, mixing, sendb, recvb, qmat, rt, lb, lt, h1, h1d, t1, vn, g1, nat, nat2, dvp, coef, outb, fgradb,
    mixs, mixr, gmacc, gms, gm1, gmy, gacc, gsend, rsr, ag,
    a_send, a_recv, m_send, m_recv, r_send, r_recv, g_send, g_recv, o_sem, i_sem,
):
    samples = h1.shape[3]
    me = lax.axis_index("chan") * 2 + lax.axis_index("bfly")
    y = lax.axis_index("samp")

    def fetch(n, src, dst):
        return pltpu.make_async_copy(src, dst, i_sem.at[n])

    fetches = [
        fetch(2, cot_hbm, cot),
        fetch(0, right_hbm.at[0], right.at[0]),
        fetch(1, feat_hbm, feat),
        fetch(3, left_hbm.at[0], left.at[0]),
        fetch(4, right_hbm.at[1], right.at[1]),
        fetch(5, left_hbm.at[1], left.at[1]),
        fetch(6, mixing_hbm, mixing),
    ]
    for one_fetch in fetches:
        one_fetch.start()
    fetches = [fetches[1], fetches[2], fetches[0]] + fetches[3:]

    def peer_id(p):
        return {"chan": p // 2, "bfly": lax.rem(p, 2)}

    barrier = pltpu.get_barrier_semaphore()

    def greet(k, carry):
        pl.semaphore_signal(barrier, inc=1, device_id=peer_id(lax.rem(me + k, PEERS)), device_id_type=MESH)
        return carry

    lax.fori_loop(1, PEERS, greet, 0)
    for d in range(1, SAMP):
        pl.semaphore_signal(barrier, inc=1, device_id={"samp": lax.rem(y + d, SAMP)}, device_id_type=MESH)

    i0 = lax.broadcasted_iota(jnp.int32, (BLOCK, BLOCK), 0)
    i1 = lax.broadcasted_iota(jnp.int32, (BLOCK, BLOCK), 1)

    def row_of(m):
        return ((m >> 2) & 3) * 64 + (m >> 4) * 4 + (m & 3)

    def col_of(m):
        return (m & 3) * 64 + (m >> 4) * 4 + ((m >> 2) & 3)

    def onehot(mask):
        return jnp.where(mask, 1.0, 0.0).astype(BF16)

    qmat[Q_ROW] = onehot(i1 == row_of(i0))

    def to_peers(which, src, put):
        for g in range(GROUPS):
            x = jnp.concatenate([src[b, 64 * g : 64 * g + 64, :] for b in range(OWN)], axis=0)
            put(g, mm(qmat[which], x))

    def put_into(dst):
        def put(g, value):
            dst[GPEERS * g : GPEERS * (g + 1)] = value.astype(BF16).reshape(GPEERS, ROWS, samples)

        return put

    def split_into(dst, g, value):
        value = value.astype(BF16)
        for b in range(OWN):
            dst[b, 64 * g : 64 * g + 64, :] = value[64 * b : 64 * b + 64]

    def from_peers(which, src, dst):
        for g in range(GROUPS):
            x = src[GPEERS * g : GPEERS * (g + 1)].reshape(BLOCK, samples)
            split_into(dst, g, mm(qmat[which], x))

    def chunk_of(c):
        return pl.ds(pl.multiple_of(c * samples, samples), samples)

    def send(a, c, low=1, high=PEERS):
        def one(k, carry):
            p = lax.rem(me + k, PEERS)
            pltpu.make_async_remote_copy(
                src_ref=sendb.at[a, c, p], dst_ref=recvb.at[a, c, me],
                send_sem=a_send.at[a, c], recv_sem=a_recv.at[a, c],
                device_id=peer_id(p), device_id_type=MESH,
            ).start()
            return carry

        lax.fori_loop(low, high, one, 0)
        if low == 1:
            recvb[a, c, pl.ds(me, 1)] = sendb[a, c, pl.ds(me, 1)]

    def wait_all(ref, sem):
        pltpu.make_async_copy(ref, ref, sem).wait()

    def wait_recv(a, c):
        wait_all(recvb.at[a, c, pl.ds(0, PEERS - 1)], a_recv.at[a, c])

    def first(c):
        for b in range(OWN):
            nat[b] = mm(rt[0, b], feat[b, :, chunk_of(c)]).astype(BF16)
        to_peers(Q_ROW, nat, put_into(sendb.at[U1, c]))

    def first_cot(c):
        for b in range(OWN):
            nat2[b] = cot[b, :, chunk_of(c)]
        to_peers(Q_ROW, nat2, put_into(sendb.at[COT, c]))

    fetches[2].wait()
    first_cot(0)
    pl.semaphore_wait(barrier, PEERS - 1 + SAMP - 1)
    send(COT, 0)
    fetches[0].wait()
    for b in range(OWN):
        rt[0, b] = right[0, b].T
    fetches[1].wait()
    first(0)
    send(U1, 0)

    pick = onehot((lax.broadcasted_iota(jnp.int32, (BLOCK, 128), 0) & 3) == (lax.broadcasted_iota(jnp.int32, (BLOCK, 128), 1) & 3)).astype(F32)
    lane = lax.broadcasted_iota(jnp.int32, (PEERS, 128), 1)
    owner = lax.broadcasted_iota(jnp.int32, (PEERS, BLOCK), 0)
    unit = lax.broadcasted_iota(jnp.int32, (PEERS, BLOCK), 1)
    fetches[6].wait()
    message = jnp.zeros((PEERS, 128), F32)
    for r in range(ROWS):
        row = mixing[r // 8, (r // 4) % 2, r % 4 : r % 4 + 1, :]
        spread = jnp.where((unit >> 2) == owner, jnp.broadcast_to(row, (PEERS, BLOCK)), 0.0)
        found = lax.dot_general(
            spread, pick, (((1,), (0,)), ((), ())), precision=lax.Precision.HIGHEST, preferred_element_type=F32
        )
        message = message + jnp.where((lane >> 2) == r, found, 0.0)
    mixs[...] = message.reshape(PEERS, 1, 128)

    def send_mix(k, carry):
        p = lax.rem(me + k, PEERS)
        pltpu.make_async_remote_copy(
            src_ref=mixs.at[p], dst_ref=mixr.at[me], send_sem=m_send.at[0], recv_sem=m_recv.at[0],
            device_id=peer_id(p), device_id_type=MESH,
        ).start()
        return carry

    lax.fori_loop(1, PEERS, send_mix, 0)
    mixr[pl.ds(me, 1)] = mixs[pl.ds(me, 1)]
    for c in range(1, CHUNKS):
        first(c)
        send(U1, c)

    qmat[Q_ROW_T] = onehot(i0 == row_of(i1))
    qmat[Q_COL] = onehot(i1 == col_of(i0))
    qmat[Q_COL_T] = onehot(i0 == col_of(i1))
    for c in range(1, CHUNKS):
        first_cot(c)
    for n in (3, 4, 5):
        fetches[n].wait()
    for b in range(OWN):
        rt[1, b] = right[1, b].T
        for layer in range(LAYERS):
            lb[layer, b] = left[layer, b].astype(BF16)
            lt[layer, b] = left[layer, b].T.astype(BF16)
    for a in range(4):
        gacc[a] = jnp.zeros((OWN, BLOCK, BLOCK), F32)
    gmacc[...] = jnp.zeros((PEERS, 128), F32)
    wait_all(mixr.at[pl.ds(0, PEERS - 1)], m_recv.at[0])
    lane3 = lax.broadcasted_iota(jnp.int32, (GPEERS, ROWS, 128), 2)
    row3 = lax.broadcasted_iota(jnp.int32, (GPEERS, ROWS, 128), 1)
    for g in range(GROUPS):
        got = jnp.broadcast_to(mixr[GPEERS * g : GPEERS * (g + 1)], (GPEERS, ROWS, 128))
        for term in range(4):
            value = jnp.sum(jnp.where(lane3 == row3 + ROWS * term, got, 0.0), axis=2, keepdims=True)
            coef[term, GPEERS * g : GPEERS * (g + 1)] = jnp.broadcast_to(value, (GPEERS, ROWS, 128))

    def gain(term, g):
        value = coef[term, GPEERS * g : GPEERS * (g + 1)]
        return jnp.concatenate([value] * (samples // 128), axis=2)

    def mix_forward(layer, a, c):
        for g in range(GROUPS):
            u = recvb[a, c, GPEERS * g : GPEERS * (g + 1)].astype(F32)
            v = (gain(2 * layer, g) * u + gain(2 * layer + 1, g) * flip(u)).astype(BF16)
            split_into(vn.at[layer, c], g, mm(qmat[Q_COL_T], v.reshape(BLOCK, samples)))

    def mix_backward(layer, a, c):
        def put(g, value):
            dv = value.reshape(GPEERS, ROWS, samples)
            dvp[GPEERS * g : GPEERS * (g + 1)] = dv.astype(BF16)
            part = (gain(2 * layer + 1, g) * dv).astype(BF16).astype(F32)
            du = gain(2 * layer, g) * dv + flip(part)
            sendb[a, c, GPEERS * g : GPEERS * (g + 1)] = du.astype(BF16)

        to_peers(Q_COL, nat2, put)

    def mix_gradient(layer, a, c):
        for g in range(GROUPS):
            dv = dvp[GPEERS * g : GPEERS * (g + 1)].astype(F32)
            u = recvb[a, c, GPEERS * g : GPEERS * (g + 1)].astype(F32)
            total = jnp.zeros((GPEERS, ROWS, 128), F32)
            for term, other in ((0, u), (1, flip(u))):
                prod = dv * other
                half = prod[:, :, :128]
                for piece in range(1, samples // 128):
                    half = half + prod[:, :, 128 * piece : 128 * (piece + 1)]
                value = jnp.sum(half, axis=2, keepdims=True)
                total = total + jnp.where(
                    lane3 == row3 + ROWS * (2 * layer + term), jnp.broadcast_to(value, (GPEERS, ROWS, 128)), 0.0
                )
            gmacc[GPEERS * g : GPEERS * (g + 1)] += jnp.sum(total, axis=1)

    def scatter(a):
        gsend[a] = gacc[a].astype(BF16)
        for d in range(1, SAMP):
            to = lax.rem(y + d, SAMP)
            pltpu.make_async_remote_copy(
                src_ref=gsend.at[a, to], dst_ref=rsr.at[a, y], send_sem=r_send.at[a], recv_sem=r_recv.at[a],
                device_id={"samp": to}, device_id_type=MESH,
            ).start()

    def gather(a):
        wait_all(rsr.at[a, pl.ds(0, SAMP - 1)], r_recv.at[a])
        total = gacc[a, y]
        for d in range(1, SAMP):
            total = total + rsr[a, lax.rem(y + d, SAMP)].astype(F32)
        ag[a, y] = total.astype(BF16)
        for d in range(1, SAMP):
            to = lax.rem(y + d, SAMP)
            pltpu.make_async_remote_copy(
                src_ref=ag.at[a, y], dst_ref=ag.at[a, y], send_sem=g_send.at[a], recv_sem=g_recv.at[a],
                device_id={"samp": to}, device_id_type=MESH,
            ).start()

    def store(a):
        wait_all(ag.at[a, pl.ds(0, SAMP - 1)], g_recv.at[a])
        dst = (gleft_hbm if a in (GL1, GL2) else gright_hbm).at[0 if a in (GL1, GR1) else 1]
        pltpu.make_async_copy(ag.at[a], dst, o_sem.at[a]).start()

    def col1(c, carry):
        wait_recv(U1, c)
        mix_forward(0, U1, c)
        for j in range(OWN):
            nat[j] = mm(lt[0, j], vn[0, c, j]).astype(BF16)
        to_peers(Q_COL, nat, put_into(sendb.at[T1, c]))
        send(T1, c)
        return carry

    lax.fori_loop(0, CHUNKS, col1, 0)
    for c in range(1, CHUNKS):
        send(COT, c)

    def row2(c, carry):
        wait_recv(T1, c)
        from_peers(Q_ROW_T, recvb.at[T1, c], t1.at[c])
        for b in range(OWN):
            t = t1[c, b].astype(F32)
            h = (feat[b, :, chunk_of(c)].astype(F32) + t * jax.nn.sigmoid(t)).astype(BF16)
            h1[c, b] = h
            nat[b] = mm(rt[1, b], h).astype(BF16)
        to_peers(Q_ROW, nat, put_into(sendb.at[U2, c]))
        send(U2, c)
        return carry

    lax.fori_loop(0, CHUNKS, row2, 0)

    def slope(g, t):
        s = jax.nn.sigmoid(t)
        return (g * s * (1.0 + t * (1.0 - s))).astype(BF16)

    def col2(c):
        wait_recv(COT, c)
        from_peers(Q_COL_T, recvb.at[COT, c], nat2)
        wait_recv(U2, c)
        mix_forward(1, U2, c)
        for j in range(OWN):
            t = mm(lt[1, j], vn[1, c, j]).astype(BF16)
            nat[j] = t
            e = slope(nat2[j].astype(F32), t.astype(F32))
            gacc[GL2, j] += mm_t(vn[1, c, j], e)
            nat2[j] = mm(lb[1, j], e).astype(BF16)
        if c == CHUNKS - 1:
            scatter(GL2)
        mix_backward(1, DU2, c)
        send(DU2, c)
        to_peers(Q_COL, nat, put_into(sendb.at[T2, c]))
        mix_gradient(1, U2, c)

    for c in range(CHUNKS):
        col2(c)

    def row1(c):
        wait_recv(DU2, c)
        from_peers(Q_ROW_T, recvb.at[DU2, c], nat)
        for b in range(OWN):
            g = (cot[b, :, chunk_of(c)].astype(F32) + mm(right[1, b], nat[b])).astype(BF16)
            g1[c, b] = g
            nat2[b] = slope(g.astype(F32), t1[c, b].astype(F32))
        to_peers(Q_ROW, nat2, put_into(sendb.at[E1, c]))

    def row1_grad(c):
        for b in range(OWN):
            gacc[GR2, b] += mm_t(h1[c, b], nat[b])

    row1(0)
    send(E1, 0)
    row1_grad(0)
    gather(GL2)
    row1(1)
    row1_grad(1)
    scatter(GR2)
    send(E1, 1)

    def col1_back(c):
        wait_recv(E1, c)
        from_peers(Q_COL_T, recvb.at[E1, c], nat)
        for j in range(OWN):
            nat2[j] = mm(lb[0, j], nat[j]).astype(BF16)
        mix_backward(0, DU1, c)

    def col1_grad(c):
        for j in range(OWN):
            gacc[GL1, j] += mm_t(vn[0, c, j], nat[j])

    col1_back(0)
    send(DU1, 0)
    col1_grad(0)
    mix_gradient(0, U1, 0)
    gather(GR2)
    col1_back(1)
    col1_grad(1)
    scatter(GL1)
    send(DU1, 1)
    mix_gradient(0, U1, 1)
    store(GL2)
    gms[...] = gmacc[...].reshape(PEERS, 1, 128)

    def send_gm(k, carry):
        p = lax.rem(me + k, PEERS)
        pltpu.make_async_remote_copy(
            src_ref=gms.at[p], dst_ref=gm1.at[me], send_sem=m_send.at[1], recv_sem=m_recv.at[1],
            device_id=peer_id(p), device_id_type=MESH,
        ).start()
        return carry

    lax.fori_loop(1, PEERS, send_gm, 0)
    gm1[pl.ds(me, 1)] = gms[pl.ds(me, 1)]
    store(GR2)
    gather(GL1)
    send(T2, 0)

    dun = h1d

    def row0(c, carry):
        wait_recv(DU1, c)
        from_peers(Q_ROW_T, recvb.at[DU1, c], dun.at[c])
        for b in range(OWN):
            gacc[GR1, b] += mm_t(feat[b, :, chunk_of(c)], dun[c, b])
        return carry

    row0(0, 0)
    last = CHUNKS - 1
    wait_recv(DU1, last)
    from_peers(Q_ROW_T, recvb.at[DU1, last], dun.at[last])
    for d in range(1, SAMP + 1):
        to = lax.rem(y + d, SAMP)
        gacc[GR1, to] += mm_t(feat[to, :, chunk_of(last)], dun[last, to])
        if d < SAMP:
            gsend[GR1, to] = gacc[GR1, to].astype(BF16)
            pltpu.make_async_remote_copy(
                src_ref=gsend.at[GR1, to], dst_ref=rsr.at[GR1, y], send_sem=r_send.at[GR1], recv_sem=r_recv.at[GR1],
                device_id={"samp": to}, device_id_type=MESH,
            ).start()
    wait_all(gm1.at[pl.ds(0, PEERS - 1)], m_recv.at[1])
    gmy[pl.ds(y, 1)] = gm1[...].reshape(1, PEERS, 1, 128)
    for d in range(1, SAMP):
        to = lax.rem(y + d, SAMP)
        pltpu.make_async_remote_copy(
            src_ref=gm1, dst_ref=gmy.at[y], send_sem=r_send.at[4], recv_sem=r_recv.at[4],
            device_id={"samp": to}, device_id_type=MESH,
        ).start()
    send(T2, 1, 1, TAIL_CUT)

    def row0_grad(c, carry):
        for b in range(OWN):
            fgradb[b, :, chunk_of(c)] = (g1[c, b].astype(F32) + mm(right[0, b], dun[c, b])).astype(BF16)
        return carry

    lax.fori_loop(0, CHUNKS, row0_grad, 0)
    pltpu.make_async_copy(fgradb, fgrad_hbm, o_sem.at[5]).start()
    store(GL1)
    gather(GR1)
    send(T2, 1, TAIL_CUT, PEERS)
    wait_all(gmy.at[pl.ds(0, SAMP - 1)], r_recv.at[4])
    total = (gmy[0] + gmy[1] + gmy[2] + gmy[3]).reshape(PEERS, 128)
    spread_back = onehot(
        (lax.broadcasted_iota(jnp.int32, (128, BLOCK), 0) & 3) == (lax.broadcasted_iota(jnp.int32, (128, BLOCK), 1) & 3)
    ).astype(F32)
    for r in range(ROWS):
        found = lax.dot_general(
            jnp.where((lane >> 2) == r, total, 0.0), spread_back, (((1,), (0,)), ((), ())),
            precision=lax.Precision.HIGHEST, preferred_element_type=F32,
        )
        gmix_ref[r // 8, (r // 4) % 2, r % 4 : r % 4 + 1, :] = jnp.sum(
            jnp.where((unit >> 2) == owner, found, 0.0), axis=0, keepdims=True
        )

    def final_output(c, carry):
        wait_recv(T2, c)
        from_peers(Q_ROW_T, recvb.at[T2, c], nat)
        for b in range(OWN):
            t = nat[b].astype(F32)
            outb[b, :, chunk_of(c)] = (h1[c, b].astype(F32) + t * jax.nn.sigmoid(t)).astype(BF16)
        return carry

    final_output(0, 0)
    store(GR1)
    final_output(1, 0)
    pltpu.make_async_copy(outb, out_hbm, o_sem.at[4]).start()

    for a in range(8):
        for c in range(CHUNKS):
            wait_all(sendb.at[a, c, pl.ds(0, PEERS - 1)], a_send.at[a, c])
    wait_all(mixs.at[pl.ds(0, PEERS - 1)], m_send.at[0])
    wait_all(gms.at[pl.ds(0, PEERS - 1)], m_send.at[1])
    for a in range(4):
        wait_all(rsr.at[a, pl.ds(0, SAMP - 1)], r_send.at[a])
        wait_all(ag.at[a, pl.ds(0, SAMP - 1)], g_send.at[a])
        wait_all(ag.at[a], o_sem.at[a])
    wait_all(gmy.at[pl.ds(0, SAMP - 1)], r_send.at[4])
    wait_all(outb, o_sem.at[4])
    wait_all(fgradb, o_sem.at[5])


def finish(out_in, fgrad_in, gright_in, gleft_in, gmix_in, out, fgrad, gright, gleft, gmix, wide, sem):
    whole = [
        pltpu.make_async_copy(src, dst, sem.at[0, n])
        for n, (src, dst) in enumerate(((out_in, out), (fgrad_in, fgrad), (gmix_in, gmix)))
    ]
    for copy in whole:
        copy.start()
    pieces = []
    for n, (src, dst) in enumerate(((gright_in, gright), (gleft_in, gleft))):
        for layer in range(LAYERS):
            for b in range(OWN):
                wide[n, layer, b] = src[layer, b].astype(F32)
                copy = pltpu.make_async_copy(wide.at[n, layer, b], dst.at[layer, b], sem.at[1 + n, OWN * layer + b])
                copy.start()
                pieces.append(copy)
    for copy in whole + pieces:
        copy.wait()


def local(features, cotangent, right_factor, left_factor, mixing):
    width = features.shape[1]
    samples = width // CHUNKS
    vmem = pl.BlockSpec(memory_space=pltpu.VMEM)
    hbm = pl.BlockSpec(memory_space=pl.ANY)
    acts = jax.ShapeDtypeStruct((OWN, BLOCK, width), BF16)
    grads = jax.ShapeDtypeStruct((LAYERS, OWN, BLOCK, BLOCK), BF16)
    chunked = pltpu.VMEM((CHUNKS, OWN, BLOCK, samples), BF16)
    small = pltpu.VMEM((PEERS, 1, 128), F32)
    output, fgrad, gright, gleft, gmix = pl.pallas_call(
        kernel,
        out_shape=(acts, acts, grads, grads, jax.ShapeDtypeStruct((LAYERS, 2, OWN, BLOCK), F32)),
        in_specs=[pl.BlockSpec(memory_space=pltpu.HBM)] * 5,
        out_specs=(hbm, hbm, hbm, hbm, vmem),
        scratch_shapes=[
            pltpu.VMEM((OWN, BLOCK, width), BF16),
            pltpu.VMEM((OWN, BLOCK, width), BF16),
            pltpu.VMEM((LAYERS, OWN, BLOCK, BLOCK), BF16),
            pltpu.VMEM((LAYERS, OWN, BLOCK, BLOCK), F32),
            pltpu.VMEM((LAYERS, 2, OWN, BLOCK), F32),
            pltpu.VMEM((8, CHUNKS, PEERS, ROWS, samples), BF16),
            pltpu.VMEM((8, CHUNKS, PEERS, ROWS, samples), BF16),
            pltpu.VMEM((4, BLOCK, BLOCK), BF16),
            pltpu.VMEM((LAYERS, OWN, BLOCK, BLOCK), BF16),
            pltpu.VMEM((LAYERS, OWN, BLOCK, BLOCK), BF16),
            pltpu.VMEM((LAYERS, OWN, BLOCK, BLOCK), BF16),
            chunked,
            chunked,
            chunked,
            pltpu.VMEM((LAYERS, CHUNKS, OWN, BLOCK, samples), BF16),
            chunked,
            pltpu.VMEM((OWN, BLOCK, samples), BF16),
            pltpu.VMEM((OWN, BLOCK, samples), BF16),
            pltpu.VMEM((PEERS, ROWS, samples), BF16),
            pltpu.VMEM((4, PEERS, ROWS, 128), F32),
            pltpu.VMEM((OWN, BLOCK, width), BF16),
            pltpu.VMEM((OWN, BLOCK, width), BF16),
            small,
            small,
            pltpu.VMEM((PEERS, 128), F32),
            small,
            small,
            pltpu.VMEM((SAMP, PEERS, 1, 128), F32),
            pltpu.VMEM((4, OWN, BLOCK, BLOCK), F32),
            pltpu.VMEM((4, OWN, BLOCK, BLOCK), BF16),
            pltpu.VMEM((4, SAMP, BLOCK, BLOCK), BF16),
            pltpu.VMEM((4, SAMP, BLOCK, BLOCK), BF16),
            pltpu.SemaphoreType.DMA((8, CHUNKS)),
            pltpu.SemaphoreType.DMA((8, CHUNKS)),
            pltpu.SemaphoreType.DMA((2,)),
            pltpu.SemaphoreType.DMA((2,)),
            pltpu.SemaphoreType.DMA((5,)),
            pltpu.SemaphoreType.DMA((5,)),
            pltpu.SemaphoreType.DMA((4,)),
            pltpu.SemaphoreType.DMA((4,)),
            pltpu.SemaphoreType.DMA((6,)),
            pltpu.SemaphoreType.DMA((7,)),
        ],
        compiler_params=pltpu.CompilerParams(
            collective_id=0, has_side_effects=True, vmem_limit_bytes=48 * 1024 * 1024
        ),
    )(
        *(
            pltpu.with_memory_space_constraint(value, pltpu.HBM)
            for value in (
                features.reshape(OWN, BLOCK, width),
                cotangent.reshape(OWN, BLOCK, width),
                right_factor,
                left_factor,
                mixing,
            )
        )
    )
    wide = jax.ShapeDtypeStruct((LAYERS, OWN, BLOCK, BLOCK), F32)
    output, fgrad, gright, gleft, gmix = pl.pallas_call(
        finish,
        out_shape=(acts, acts, wide, wide, jax.ShapeDtypeStruct((LAYERS, 2, OWN, BLOCK), F32)),
        in_specs=[hbm, hbm, vmem, vmem, hbm],
        out_specs=[hbm] * 5,
        scratch_shapes=[
            pltpu.VMEM((2, LAYERS, OWN, BLOCK, BLOCK), F32),
            pltpu.SemaphoreType.DMA((3, LAYERS * OWN)),
        ],
        compiler_params=pltpu.CompilerParams(vmem_limit_bytes=12 * 1024 * 1024),
    )(output, fgrad, gright, gleft, gmix)
    return output.reshape(OWN * BLOCK, width), fgrad.reshape(OWN * BLOCK, width), gright, gleft, gmix


def solution(mesh):
    specs = (
        P(("chan", "bfly"), "samp"),
        P(("chan", "bfly"), "samp"),
        P(None, ("chan", "bfly"), None, None),
        P(None, ("chan", "bfly"), None, None),
        P(None, None, ("chan", "bfly"), None),
    )
    return jax.shard_map(local, mesh=mesh, in_specs=specs, out_specs=specs, check_vma=False)
```
